128 devices in a mesh: gx: 16 (over z, y), gy: 8 (over x, core).
Axes of the slice: x: 4, y: 4, z: 4, core: 2. Of those that a mesh axis runs over, the one named last changes fastest.
Arguments:
- state: float32 [5, 120, 65536], P(None, None, ('gx', 'gy')), may hold values from -6 to 6
- coef: float32 [5, 5, 65536], P(None, None, ('gx', 'gy')), may hold values from -3 to 3
- basis_quad: float32 [216, 120], replicated, may hold values from -0.5 to 0.5
- test_deriv: float32 [120, 216], replicated, may hold values from -0.3125 to 0.3125
- trace_vec: float32 [120], replicated, may hold values from -0.5 to 0.5
- lift_vec: float32 [120], replicated, may hold values from -3 to 3
- tent_height: float32 [3, 8192], P(None, ('gx', 'gy')), may hold values from 0.2 to 0.4
- elem_tent: int32 [3, 65536], P(None, ('gx', 'gy')), may hold values from 0 to 8191, as said below
Outputs:
- final_state: float32 [5, 120, 65536], P(None, None, ('gx', 'gy'))
The draws below stay inside these ranges and needn't reach their ends.
Inputs may be any that keep to these rules, and one draw needn't show every extreme that they name: `elem_tent`: tent t is owned by device t // 64 of the devices numbered with gx slowest. At every level the owner of an element's tent is the element's own device or one of its four neighbours along gx or gy, with wrap-around. At a level no device hands more than 64 of its elements to one neighbour; in every level some device hands exactly 64 to a neighbour, and some device receives exactly 64 from each of its four neighbours.
All inputs are finite; a program needn't handle non-finite values.
Results may differ from the reference program's by a relative error of at most 0.00011.
Values sent between devices are 32-bit elements; how exact they have to be, the bound alone decides.
No kernel may reach another device: no remote copies, remote signals or barrier semaphores. Data moves between devices by JAX's collectives and lax.ppermute only.
A program may use at most 128 MiB of HBM per device.

```python
import jax
import jax.numpy as jnp
from jax import lax

NF = 5
NB = 120
NQ = 216
E_DEV = 512
LEVELS = 3
CAP = 64
TENT_DEV = 64
ELEMS = 65536
TENTS = 8192
N_GX = 16
N_GY = 8


def draw_elem_tent(key, part):
    devices_all = N_GX * N_GY
    rows_all = []
    step_first = jnp.array([1, -1, 0, 0, 0], dtype=jnp.int32)
    step_second = jnp.array([0, 0, 1, -1, 0], dtype=jnp.int32)
    for level_index in range(LEVELS):
        level_key = jax.random.fold_in(key, 7919 + level_index)
        key_counts, key_target, key_order, key_local = jax.random.split(level_key, 4)
        handed = jax.random.randint(key_counts, (devices_all, 4), CAP // 2, CAP + 1)
        target = jax.random.randint(key_target, (), 0, devices_all)
        target_first = target // N_GY
        target_second = target % N_GY
        senders = jnp.stack([(target_first - 1) % N_GX * N_GY + target_second, (target_first + 1) % N_GX * N_GY + target_second, target_first * N_GY + (target_second - 1) % N_GY, target_first * N_GY + (target_second + 1) % N_GY])
        handed = handed.at[senders, jnp.arange(4)].set(CAP)
        ranks = jax.vmap(lambda single: jax.random.permutation(single, E_DEV))(jax.random.split(key_order, devices_all))
        bounds = jnp.cumsum(handed, axis=1)
        heading = jnp.sum((ranks[:, :, None] >= bounds[:, None, :]).astype(jnp.int32), axis=2)
        device_ids = jnp.arange(devices_all, dtype=jnp.int32)
        place_first = device_ids // N_GY
        place_second = device_ids % N_GY
        owner_first = (place_first[:, None] + step_first[heading]) % N_GX
        owner_second = (place_second[:, None] + step_second[heading]) % N_GY
        owner = owner_first * N_GY + owner_second
        local_tent = jax.random.randint(key_local, (devices_all, E_DEV), 0, TENT_DEV)
        rows_all.append((owner * TENT_DEV + local_tent).reshape(-1))
    return jnp.stack(rows_all).astype(jnp.int32)


def block_levels(rng, dims, cuts, least, high):
    def one(dim, shards_of):
        steps = jax.random.uniform(jax.random.fold_in(jax.random.fold_in(rng, 6), dim), (shards_of,), jnp.float32, least / len(cuts), high / len(cuts))
        return jnp.repeat(jnp.exp(steps), dims[dim] // shards_of).reshape((-1,) + (1,) * (len(dims) - dim - 1))

    level = one(*cuts[0])
    for cut in cuts[1:]:
        level = level * one(*cut)
    return level


def scatter_about(rng, dims, deviation, most, cuts=(), kind=jnp.bfloat16):
    values = jax.random.normal(rng, dims, jnp.float32) * deviation
    if len(cuts) > 0:
        values = block_levels(rng, dims, cuts, -0.22, 0.18) * values
    return jnp.clip(values, min=-most, max=most).astype(kind)


def setup_inputs(seed: int = 0) -> dict:
    keys = jax.random.split(jax.random.key(seed), 9)
    state = scatter_about(keys[0], (NF, NB, ELEMS), 1.0, 6.0, ((2, 128),), jnp.float32)
    coef = scatter_about(keys[1], (NF, NF, ELEMS), 0.45, 3.0, ((2, 128),), jnp.float32)
    basis_quad = scatter_about(keys[2], (NQ, NB), NB ** -0.5, 0.5, (), jnp.float32)
    test_deriv = scatter_about(keys[3], (NB, NQ), (2 * NQ) ** -0.5, 0.3125, (), jnp.float32)
    trace_vec = scatter_about(keys[4], (NB,), NB ** -0.5, 0.5, (), jnp.float32)
    lift_vec = scatter_about(keys[5], (NB,), 0.5, 3.0, (), jnp.float32)
    tent_height = jnp.clip(0.2 + 0.2 * jax.random.uniform(keys[6], (LEVELS, TENTS), jnp.float32) ** block_levels(keys[6], (LEVELS, TENTS), ((1, 128),), -0.2, 0.2), 0.2, 0.4)
    elem_tent = draw_elem_tent(jax.random.fold_in(keys[8], 71), 0)
    return {"state": state, "coef": coef, "basis_quad": basis_quad, "test_deriv": test_deriv, "trace_vec": trace_vec, "lift_vec": lift_vec, "tent_height": tent_height, "elem_tent": elem_tent}


def reference(state, coef, basis_quad, test_deriv, trace_vec, lift_vec, tent_height, elem_tent):
    highest = lax.Precision.HIGHEST
    values = state
    for level_index in range(LEVELS):
        tents = elem_tent[level_index]
        counts = jax.ops.segment_sum(jnp.ones(tents.shape, jnp.float32), tents, TENTS)
        safe_counts = jnp.maximum(counts, 1.0)
        heights = tent_height[level_index][tents][None, None, :]

        def derivative(current):
            traces = jnp.einsum("b,fbs->fs", trace_vec, current, precision=highest)
            sums = jax.ops.segment_sum(traces.T, tents, TENTS)
            means = (sums / safe_counts[:, None])[tents].T
            at_points = jnp.einsum("qb,fbs->fqs", basis_quad, current, precision=highest)
            flux_all = jnp.einsum("gfs,fqs->gqs", coef, at_points, precision=highest)
            weak_form = jnp.einsum("bq,gqs->gbs", test_deriv, flux_all, precision=highest)
            return weak_form + lift_vec[None, :, None] * (means - traces)[:, None, :]

        first = derivative(values)
        second = derivative(first)
        third = derivative(second)
        values = values + heights * first + heights * heights / 2.0 * second + heights * heights * heights / 6.0 * third
    return values
```

```python
import functools

import jax
import jax.numpy as jnp
from jax import lax
from jax.experimental import pallas as pl
from jax.experimental.pallas import tpu as pltpu
from jax.sharding import PartitionSpec as P

F32 = jnp.float32
BF16 = jnp.bfloat16
HIGHEST = lax.Precision.HIGHEST
ROWS = 48
BACK = 16
SLOTS = 5


def split(x):
    high = x.astype(BF16)
    return high, (x - high.astype(F32)).astype(BF16)


def exact_dot(left, right):
    return jnp.dot(left, right, precision=HIGHEST, preferred_element_type=F32)


def dot_rows(left, right):
    return lax.dot_general(
        left, right, (((1,), (1,)), ((), ())), precision=HIGHEST, preferred_element_type=F32
    )


def partners(index, size):
    even = index + 1 - 2 * lax.rem(index, 2)
    odd = lax.rem(index - 1 + 2 * lax.rem(index, 2) + size, size)
    return even, odd


def tent_columns(tents, me, size_first, size_second, tent_dev):
    first = lax.div(me, size_second)
    second = lax.rem(me, size_second)
    first_even, first_odd = partners(first, size_first)
    second_even, second_odd = partners(second, size_second)
    owners = [
        first_even * size_second + second,
        first_odd * size_second + second,
        first * size_second + second_even,
        first * size_second + second_odd,
    ]
    column = tents - (me - 4) * tent_dev
    for slot, owner in enumerate(owners):
        inside = (tents >= owner * tent_dev) & (tents < (owner + 1) * tent_dev)
        column = jnp.where(inside, tents - (owner - slot) * tent_dev, column)
    return column


def members(tents, me, shape):
    size_first, size_second, tent_dev = shape
    column = tent_columns(tents, me, size_first, size_second, tent_dev)
    full = (SLOTS * tent_dev, column.shape[1])
    lines = lax.broadcasted_iota(jnp.int32, full, 0)
    return jnp.where(lines == column, 1.0, 0.0).astype(BF16)


def mix(coef, values):
    mixed = []
    for target in range(len(values)):
        total = coef[target, 0:1, :] * values[0]
        for source in range(1, len(values)):
            total = total + coef[target, source : source + 1, :] * values[source]
        mixed.append(total)
    return mixed


def tent_sums(coef, member, traces, aux, vals, messages, heights, kappa):
    fields = len(traces)
    once = mix(coef, traces)
    twice = mix(coef, once)
    vals[...] = jnp.zeros_like(vals)
    aux[...] = jnp.zeros_like(aux)
    for f in range(fields):
        vals[f : f + 1, :] = traces[f][0:1]
        vals[5 + f : 6 + f, :] = once[f][1:2]
        vals[10 + f : 11 + f, :] = twice[f][2:3] - kappa * once[f][0:1]
        vals[15 + 5 * f : 20 + 5 * f, :] = coef[f]
        aux[f : f + 1, :] = traces[f][0:1]
        aux[5 + f : 6 + f, :] = once[f][1:2]
        aux[10 + f : 11 + f, :] = twice[f][2:3]
    vals[40:41, :] = jnp.ones_like(vals[40:41, :])
    high, low = split(vals[...])
    both = jnp.concatenate([high, low], axis=0)
    sums = lax.dot_general(
        both, member, (((1,), (1,)), ((), ())), preferred_element_type=F32
    )
    sums = sums[:ROWS] + sums[ROWS:]
    tent_dev = messages[0].shape[1]
    for slot in range(SLOTS):
        messages[slot][...] = sums[:, slot * tent_dev : (slot + 1) * tent_dev]
        if heights is not None:
            messages[slot][41:44, :] = heights[...]


def opening_kernel(shape, me, basis, test, trace, lift, state, coef, heights, tents, *rest):
    smat, rows3, aux, *messages = rest[:-1]
    vals = rest[-1]
    s = exact_dot(test[...], basis[...])
    smat[...] = s
    t0 = trace[...]
    t1 = exact_dot(t0, s)
    t2 = exact_dot(t1, s)
    rows3[...] = jnp.zeros_like(rows3)
    rows3[0:1, :] = t0
    rows3[1:2, :] = t1
    rows3[2:3, :] = t2
    kappa = jnp.sum(t1 * lift[...], axis=1, keepdims=True)
    columns = rows3[...].T
    wide = [
        jnp.broadcast_to(columns[:, k : k + 1], (columns.shape[0], 128)) for k in range(3)
    ]
    fields = state.shape[0]
    traces = []
    for f in range(fields):
        parts = []
        for lane in range(state.shape[2] // 128):
            block = state[f, :, lane * 128 : (lane + 1) * 128]
            parts.append(
                jnp.concatenate(
                    [jnp.sum(block * wide[k], axis=0, keepdims=True) for k in range(3)], axis=0
                )
            )
        traces.append(jnp.concatenate(parts, axis=1))
    member = members(tents[0:1, :], me[0], shape)
    tent_sums(coef, member, traces, aux, vals, messages, heights, kappa)


def powers_kernel(smat, rows3, lift, state, stack, lcols, kappas, projections, rows, lrows):
    basis = smat.shape[0]
    s1 = smat[...]
    s2 = exact_dot(s1, s1)
    s3 = exact_dot(s2, s1)
    s4 = exact_dot(s2, s2)
    stack[...] = jnp.zeros_like(stack)
    half = stack.shape[1] // 2
    for power, matrix in enumerate((s1, s2, s3)):
        high, low = split(matrix)
        for side in range(2):
            stack[power * half : power * half + basis, side * half : side * half + basis] = high
            stack[
                (3 + power) * half : (3 + power) * half + basis,
                side * half : side * half + basis,
            ] = low
    rows[...] = jnp.zeros_like(rows)
    lrows[...] = jnp.zeros_like(lrows)
    rows[0:2, :] = rows3[0:2, :]
    rows[2:4, :] = exact_dot(rows3[0:2, :], s2)
    rows[4:8, :] = exact_dot(rows[0:4, :], s4)
    rows[8:9, :] = exact_dot(rows[4:5, :], s4)
    lrows[0:1, :] = lift[...]
    lrows[1:2, :] = dot_rows(lift[...], s1)
    lrows[2:4, :] = dot_rows(lrows[0:2, :], s2)
    lrows[4:8, :] = dot_rows(lrows[0:4, :], s4)
    lrows[8:9, :] = dot_rows(lrows[4:5, :], s4)
    lcols[...] = lrows[...].T
    kappas[...] = jnp.broadcast_to(
        jnp.sum(rows[...] * lift[...], axis=1, keepdims=True), kappas.shape
    )
    for f in range(state.shape[0]):
        projections[f] = exact_dot(rows[...], state[f])


def owner_kernel(kappas, own, *rest):
    *received, out = rest
    total = own[...]
    for ref in received:
        total = total + ref[...]
    mean = total / jnp.maximum(total[40:41], 1.0)
    first = mean[0:5]
    out[...] = jnp.zeros_like(out)
    out[0:10, :] = mean[0:10]
    kappa = kappas[1:2, 0 : out.shape[1]]
    for g in range(5):
        moved = jnp.sum(mean[15 + 5 * g : 20 + 5 * g] * first, axis=0, keepdims=True)
        out[10 + g : 11 + g, :] = mean[10 + g : 11 + g] + kappa * moved


def gather(tables, table, member):
    tent_dev = tables[0].shape[1]
    for slot in range(SLOTS):
        table[:, slot * tent_dev : (slot + 1) * tent_dev] = tables[slot]
    high, low = split(table[...])
    found = jnp.dot(
        jnp.concatenate([high, low], axis=0), member, preferred_element_type=F32
    )
    count = table.shape[0]
    return found[:count] + found[count:]


def heights_kernel(shape, me, tents, *rest):
    *messages, out, table = rest
    for level in range(tents.shape[0]):
        member = members(tents[level : level + 1, :], me[0], shape)
        found = gather([m[32:48, :] for m in messages], table, member)
        out[level : level + 1, :] = found[9 + level : 10 + level]


def lift_weights(coef, height, means, aux, kappas):
    kappa0 = kappas[0:1, :]
    kappa1 = kappas[1:2, :]
    fields = coef.shape[0]
    first = [means[f : f + 1] - aux[f : f + 1, :] for f in range(fields)]
    second = [
        means[5 + f : 6 + f] - aux[5 + f : 6 + f, :] - kappa0 * first[f] for f in range(fields)
    ]
    moved_first = mix(coef, first)
    moved_second = mix(coef, second)
    moved_twice = mix(coef, moved_first)
    half = height * height / 2.0
    sixth = height * height * height / 6.0
    weights = []
    for f in range(fields):
        third = (
            means[10 + f : 11 + f]
            - aux[10 + f : 11 + f, :]
            - kappa1 * moved_first[f]
            - kappa0 * second[f]
        )
        weights.append(
            (
                height * first[f] + half * second[f] + sixth * third,
                half * moved_first[f] + sixth * moved_second[f],
                sixth * moved_twice[f],
            )
        )
    return weights


def element_kernel(shape, level, count, me, tents, coef, heights, kappas, old_aux, proj, *rest):
    tables = rest[:SLOTS]
    weights_out, proj_out, aux, *messages = rest[SLOTS:-2]
    vals, table = rest[-2:]
    fields = coef.shape[0]
    member = members(tents[level : level + 1, :], me[0], shape)
    means = gather([t[...] for t in tables], table, member)
    height = heights[level : level + 1, :]
    weights = lift_weights(coef, height, means, old_aux, kappas)
    weights_out[...] = jnp.zeros_like(weights_out)
    for f in range(fields):
        for k in range(3):
            weights_out[f, k : k + 1, :] = weights[f][k]
    state = mix(coef, [proj[f, 3 : 3 + count, :] for f in range(fields)])
    state = [proj[f, 2 : 2 + count, :] + height / 3.0 * state[f] for f in range(fields)]
    state = mix(coef, state)
    state = [proj[f, 1 : 1 + count, :] + height / 2.0 * state[f] for f in range(fields)]
    state = mix(coef, state)
    fresh = []
    for f in range(fields):
        value = proj[f, 0:count, :] + height * state[f]
        for k in range(3):
            value = value + kappas[k : k + count, :] * weights[f][k]
        fresh.append(value)
        proj_out[f, 0:count, :] = value
    following = members(tents[level + 1 : level + 2, :], me[0], shape)
    tent_sums(coef, following, [v[0:3] for v in fresh], aux, vals, messages, None, kappas[1:2, :])


def level_kernel(level, state, coef, heights, stack, out, packed, powers):
    fields, basis, n_elem = state.shape
    width = packed.shape[1]
    half = packed.shape[0] // 2
    packed[...] = jnp.zeros_like(packed)

    def columns(block, carry):
        start = pl.multiple_of(block * width, width)
        for f in range(fields):
            high, low = split(state[f, :, pl.ds(start, width)])
            packed[0:basis, :] = high
            packed[half : half + basis, :] = low
            product = jnp.dot(stack[...], packed[...], preferred_element_type=F32)
            powers[f] = product[: 3 * half] + product[3 * half :]

        def lanes(tile, inner):
            at = pl.multiple_of(start + tile * 128, 128)
            near = pl.multiple_of(tile * 128, 128)
            factor = [
                [
                    jnp.broadcast_to(coef[g, f : f + 1, pl.ds(at, 128)], (8, 128))
                    for f in range(fields)
                ]
                for g in range(fields)
            ]
            height = jnp.broadcast_to(heights[level : level + 1, pl.ds(at, 128)], (8, 128))

            def combine(values):
                mixed = []
                for g in range(fields):
                    total = factor[g][0] * values[0]
                    for f in range(1, fields):
                        total = total + factor[g][f] * values[f]
                    mixed.append(total)
                return mixed

            def lines(group, innermost):
                top = pl.multiple_of(group * 8, 8)

                def power(k, f):
                    return powers[f, pl.ds(k * half + top, 8), pl.ds(near, 128)]

                value = combine([power(2, f) for f in range(fields)])
                value = [power(1, f) + height / 3.0 * value[f] for f in range(fields)]
                value = combine(value)
                value = [power(0, f) + height / 2.0 * value[f] for f in range(fields)]
                value = combine(value)
                for f in range(fields):
                    out[f, pl.ds(top, 8), pl.ds(at, 128)] = (
                        state[f, pl.ds(top, 8), pl.ds(at, 128)] + height * value[f]
                    )
                return innermost

            return lax.fori_loop(0, basis // 8, lines, inner, unroll=3)

        return lax.fori_loop(0, width // 128, lanes, carry)

    lax.fori_loop(0, n_elem // width, columns, 0)


def advance(coef, height, held, count):
    fields = coef.shape[0]
    value = mix(coef, [held[f, 5 : 5 + count, :] for f in range(fields)])
    value = [held[f, 6 : 6 + count, :] + height / 3.0 * value[f] for f in range(fields)]
    value = mix(coef, value)
    value = [held[f, 7 : 7 + count, :] + height / 2.0 * value[f] for f in range(fields)]
    value = mix(coef, value)
    return [held[f, 8 : 8 + count, :] + height * value[f] for f in range(fields)]


def lift_kernel(state, coef, heights, weights0, weights1, lcols, out, held):
    fields, basis, n_elem = state.shape
    held[...] = jnp.zeros_like(held)
    for f in range(fields):
        held[f, 8:11, :] = weights0[f, 0:3, :]
    value = advance(coef, heights[1:2, :], held, 6)
    for f in range(fields):
        held[f, 8:14, :] = value[f]
        held[f, 8:11, :] = held[f, 8:11, :] + weights1[f, 0:3, :]
    value = advance(coef, heights[2:3, :], held, 9)
    high, low = split(lcols[...])
    left = jnp.concatenate([high, high, low], axis=1)
    for f in range(fields):
        held[f, 8:17, :] = value[f]
        right_high, right_low = split(held[f, 8:24, :])
        right = jnp.concatenate([right_high, right_low, right_high], axis=0)
        out[f] = state[f] + jnp.dot(left, right, preferred_element_type=F32)


def closing_kernel(shape, level, me, tents, coef, heights, kappas, old_aux, lcols, state, *rest):
    tables = rest[:SLOTS]
    out, table = rest[SLOTS:]
    fields, basis, n_elem = state.shape
    member = members(tents[level : level + 1, :], me[0], shape)
    means = gather([t[...] for t in tables], table, member)
    height = heights[level : level + 1, :]
    weights = lift_weights(coef, height, means, old_aux, kappas)
    wide = [jnp.broadcast_to(lcols[:, k : k + 1], (basis, 128)) for k in range(3)]
    for f in range(fields):
        for lane in range(n_elem // 128):
            at = slice(lane * 128, (lane + 1) * 128)
            value = state[f, :, at]
            for k in range(3):
                value = value + wide[k] * weights[f][k][:, at]
            out[f, :, at] = value


def call(kernel, outs, args, scratch=(), scalars=0, flops=1000000, name=None):
    specs = [
        pl.BlockSpec(memory_space=pltpu.SMEM if i < scalars else pltpu.VMEM)
        for i in range(len(args))
    ]
    single = not isinstance(outs, (list, tuple))
    shapes = [outs] if single else list(outs)
    moved = sum(4 * s.size for s in shapes) + sum(4 * a.size for a in args)
    result = pl.pallas_call(
        kernel,
        out_shape=shapes,
        in_specs=specs,
        out_specs=[pl.BlockSpec(memory_space=pltpu.VMEM)] * len(shapes),
        scratch_shapes=list(scratch),
        cost_estimate=pl.CostEstimate(flops=flops, bytes_accessed=moved, transcendentals=0),
        compiler_params=pltpu.CompilerParams(vmem_limit_bytes=40 * 1024 * 1024),
        name=name,
    )(*args)
    return result[0] if single else result


def shaped(*dims, dtype=F32):
    return jax.ShapeDtypeStruct(dims, dtype)


def swap(x, axis, odd):
    size = lax.axis_size(axis)
    pairs = []
    for i in range(size):
        mate = (i - 1 + 2 * (i % 2)) % size if odd else i + 1 - 2 * (i % 2)
        pairs.append((i, mate))
    return lax.ppermute(x, axis, pairs)


def exchange(pieces):
    far = swap(pieces[1], "gx", True)
    near = swap(pieces[3], "gy", True)
    return [swap(pieces[0], "gx", False), far, swap(pieces[2], "gy", False), near]


def per_device(state, coef, basis_quad, test_deriv, trace_vec, lift_vec, tent_height, elem_tent):
    size_first = lax.axis_size("gx")
    size_second = lax.axis_size("gy")
    fields, basis, n_elem = state.shape
    levels, tent_dev = tent_height.shape
    shape = (size_first, size_second, tent_dev)
    me = (lax.axis_index("gx") * size_second + lax.axis_index("gy")).reshape(1)
    trace = trace_vec.reshape(1, basis)
    lift = lift_vec.reshape(1, basis)
    message = [shaped(ROWS, tent_dev)] * SLOTS
    aux_shape = shaped(BACK, n_elem)
    vals = pltpu.VMEM((ROWS, n_elem), F32)
    table = pltpu.VMEM((BACK, SLOTS * tent_dev), F32)

    smat, rows3, aux, *out = call(
        functools.partial(opening_kernel, shape),
        [shaped(basis, basis), shaped(8, basis), aux_shape] + message,
        (me, basis_quad, test_deriv, trace, lift, state, coef, tent_height, elem_tent),
        [vals],
        1,
        name="opening",
    )
    stack, lcols, kappas, proj = call(
        powers_kernel,
        [
            shaped(768, 256, dtype=BF16),
            shaped(basis, 16),
            shaped(16, n_elem),
            shaped(fields, 16, n_elem),
        ],
        (smat, rows3, lift, state),
        [pltpu.VMEM((16, basis), F32), pltpu.VMEM((16, basis), F32)],
        flops=100000000,
        name="powers",
    )
    values = state
    weights = []
    heights = None
    for level in range(levels):
        received = exchange(out[:4])
        means = call(
            owner_kernel,
            shaped(BACK, tent_dev),
            (kappas, out[4], *received),
            name="owner",
        )
        back = exchange([means] * 4)
        if level == 0:
            heights = call(
                functools.partial(heights_kernel, shape),
                shaped(8, n_elem),
                (me, elem_tent, *received, out[4]),
                [table],
                1,
                flops=10000000,
                name="heights",
            )
        values = call(
            functools.partial(level_kernel, level),
            shaped(fields, basis, n_elem),
            (values, coef, heights, stack),
            [pltpu.VMEM((256, 256), BF16), pltpu.VMEM((fields, 384, 256), F32)],
            flops=3000000000,
            name="level",
        )
        if level < levels - 1:
            weight, proj, aux, *out = call(
                functools.partial(element_kernel, shape, level, 6 - 3 * level),
                [shaped(fields, 8, n_elem), shaped(fields, 8, n_elem), aux_shape] + message,
                (me, elem_tent, coef, heights, kappas, aux, proj, *back, means),
                [vals, table],
                1,
                name="element",
            )
            weights.append(weight)
    values = call(
        lift_kernel,
        shaped(fields, basis, n_elem),
        (values, coef, heights, weights[0], weights[1], lcols),
        [pltpu.VMEM((fields, 24, n_elem), F32)],
        flops=100000000,
        name="lifts",
    )
    return call(
        functools.partial(closing_kernel, shape, levels - 1),
        shaped(fields, basis, n_elem),
        (me, elem_tent, coef, heights, kappas, aux, lcols, values, *back, means),
        [table],
        1,
        name="closing",
    )


def solution(mesh):
    placed = (
        P(None, None, ("gx", "gy")),
        P(None, None, ("gx", "gy")),
        P(),
        P(),
        P(),
        P(),
        P(None, ("gx", "gy")),
        P(None, ("gx", "gy")),
    )
    return jax.shard_map(
        per_device,
        mesh=mesh,
        in_specs=placed,
        out_specs=P(None, None, ("gx", "gy")),
        check_vma=False,
    )
```

```python
import functools

import jax
import jax.numpy as jnp
from jax import lax
from jax.experimental import pallas as pl
from jax.experimental.pallas import tpu as pltpu
from jax.sharding import PartitionSpec as P


F32 = jnp.float32
BF16 = jnp.bfloat16
HIGHEST = lax.Precision.HIGHEST
ROWS = 48
BACK = 16
SLOTS = 5
HALVES = 2


def split(x):
    high = x.astype(BF16)
    return high, (x - high.astype(F32)).astype(BF16)


def exact_dot(left, right):
    return jnp.dot(left, right, precision=HIGHEST, preferred_element_type=F32)


def dot_rows(left, right):
    return lax.dot_general(
        left, right, (((1,), (1,)), ((), ())), precision=HIGHEST, preferred_element_type=F32
    )


def partners(index, size):
    even = index + 1 - 2 * lax.rem(index, 2)
    odd = lax.rem(index - 1 + 2 * lax.rem(index, 2) + size, size)
    return even, odd


def tent_columns(tents, me, size_first, size_second, tent_dev):
    first = lax.div(me, size_second)
    second = lax.rem(me, size_second)
    first_even, first_odd = partners(first, size_first)
    second_even, second_odd = partners(second, size_second)
    owners = [
        first_even * size_second + second,
        first_odd * size_second + second,
        first * size_second + second_even,
        first * size_second + second_odd,
    ]
    column = tents - (me - 4) * tent_dev
    for slot, owner in enumerate(owners):
        inside = (tents >= owner * tent_dev) & (tents < (owner + 1) * tent_dev)
        column = jnp.where(inside, tents - (owner - slot) * tent_dev, column)
    return column


def members(tents, me, shape):
    size_first, size_second, tent_dev = shape
    column = tent_columns(tents, me, size_first, size_second, tent_dev)
    full = (SLOTS * tent_dev, column.shape[1])
    lines = lax.broadcasted_iota(jnp.int32, full, 0)
    return jnp.where(lines == column, 1.0, 0.0).astype(BF16)


def mix(coef, values):
    mixed = []
    for target in range(len(values)):
        total = coef[target, 0:1, :] * values[0]
        for source in range(1, len(values)):
            total = total + coef[target, source : source + 1, :] * values[source]
        mixed.append(total)
    return mixed


def tent_sums(coef, member, traces, aux, vals, messages, heights, kappa):
    fields = len(traces)
    once = mix(coef, traces)
    twice = mix(coef, once)
    vals[...] = jnp.zeros_like(vals)
    aux[...] = jnp.zeros_like(aux)
    for f in range(fields):
        vals[f : f + 1, :] = traces[f][0:1]
        vals[5 + f : 6 + f, :] = once[f][1:2]
        vals[10 + f : 11 + f, :] = twice[f][2:3] - kappa * once[f][0:1]
        vals[15 + 5 * f : 20 + 5 * f, :] = coef[f]
        aux[f : f + 1, :] = traces[f][0:1]
        aux[5 + f : 6 + f, :] = once[f][1:2]
        aux[10 + f : 11 + f, :] = twice[f][2:3]
    vals[40:41, :] = jnp.ones_like(vals[40:41, :])
    high, low = split(vals[...])
    both = jnp.concatenate([high, low], axis=0)
    sums = lax.dot_general(
        both, member, (((1,), (1,)), ((), ())), preferred_element_type=F32
    )
    sums = sums[:ROWS] + sums[ROWS:]
    tent_dev = messages[0].shape[1]
    for slot in range(SLOTS):
        messages[slot][...] = sums[:, slot * tent_dev : (slot + 1) * tent_dev]
        if heights is not None:
            messages[slot][41:44, :] = heights[...]


def opening_kernel(shape, me, basis_in, test_in, trace_in, lift_in, state_in, coef_in, *rest):
    heights_in, tents_in, smat, rows3, lift_row, aux, *rest = rest
    messages = rest[:SLOTS]
    vals, basis, test, trace, lift, state, coef, heights, tents, sems = rest[SLOTS:]
    sources = (basis_in, test_in, trace_in, lift_in, state_in, coef_in, heights_in, tents_in)
    targets = (basis, test, trace, lift, state, coef, heights, tents)
    copies = [
        pltpu.make_async_copy(source, target, sems.at[k])
        for k, (source, target) in enumerate(zip(sources, targets))
    ]
    for copy in copies:
        copy.start()
    copies[0].wait()
    copies[1].wait()
    s = lax.dot_general(
        test[...],
        basis[...],
        (((0,), (0,)), ((), ())),
        precision=HIGHEST,
        preferred_element_type=F32,
    )
    smat[...] = s
    copies[2].wait()
    copies[3].wait()
    t0 = trace[...].reshape(1, s.shape[0])
    t1 = exact_dot(t0, s)
    t2 = exact_dot(t1, s)
    rows3[...] = jnp.zeros_like(rows3)
    rows3[0:1, :] = t0
    rows3[1:2, :] = t1
    rows3[2:3, :] = t2
    lift_row[...] = lift[...].reshape(1, s.shape[0])
    kappa = jnp.sum(t1 * lift_row[...], axis=1, keepdims=True)
    columns = rows3[...].T
    wide = [
        jnp.broadcast_to(columns[:, k : k + 1], (columns.shape[0], 128)) for k in range(3)
    ]
    copies[7].wait()
    member = members(tents[0:1, :], me[0], shape)
    copies[4].wait()
    fields = state.shape[0]
    traces = []
    for f in range(fields):
        parts = []
        for lane in range(state.shape[2] // 128):
            block = state[f, :, lane * 128 : (lane + 1) * 128]
            parts.append(
                jnp.concatenate(
                    [jnp.sum(block * wide[k], axis=0, keepdims=True) for k in range(3)], axis=0
                )
            )
        traces.append(jnp.concatenate(parts, axis=1))
    copies[5].wait()
    copies[6].wait()
    tent_sums(coef, member, traces, aux, vals, messages, heights, kappa)


def powers_kernel(smat, rows3, lift, state, stack, lcols, kappas, projections, rows, lrows):
    basis = smat.shape[0]
    s1 = smat[...]
    s2 = exact_dot(s1, s1)
    s3 = exact_dot(s2, s1)
    s4 = exact_dot(s2, s2)
    stack[...] = jnp.zeros_like(stack)
    half = stack.shape[1] // 2
    for power, matrix in enumerate((s1, s2 / 2.0, s3 / 6.0)):
        high, low = split(matrix)
        for side in range(2):
            stack[power * half : power * half + basis, side * half : side * half + basis] = high
            stack[
                (3 + power) * half : (3 + power) * half + basis,
                side * half : side * half + basis,
            ] = low
    rows[...] = jnp.zeros_like(rows)
    lrows[...] = jnp.zeros_like(lrows)
    rows[0:2, :] = rows3[0:2, :]
    rows[2:4, :] = exact_dot(rows3[0:2, :], s2)
    rows[4:8, :] = exact_dot(rows[0:4, :], s4)
    rows[8:9, :] = exact_dot(rows[4:5, :], s4)
    lrows[0:1, :] = lift[...]
    lrows[1:2, :] = dot_rows(lift[...], s1)
    lrows[2:4, :] = dot_rows(lrows[0:2, :], s2)
    lrows[4:8, :] = dot_rows(lrows[0:4, :], s4)
    lrows[8:9, :] = dot_rows(lrows[4:5, :], s4)
    lcols[...] = lrows[...].T
    kappas[...] = jnp.broadcast_to(
        jnp.sum(rows[...] * lift[...], axis=1, keepdims=True), kappas.shape
    )
    for f in range(state.shape[0]):
        projections[f] = exact_dot(rows[...], state[f])


def owner_kernel(kappas, own, *rest):
    *received, out = rest
    total = own[...]
    for ref in received:
        total = total + ref[...]
    mean = total / jnp.maximum(total[40:41], 1.0)
    first = mean[0:5]
    out[...] = jnp.zeros_like(out)
    out[0:10, :] = mean[0:10]
    kappa = kappas[1:2, 0 : out.shape[1]]
    for g in range(5):
        moved = jnp.sum(mean[15 + 5 * g : 20 + 5 * g] * first, axis=0, keepdims=True)
        out[10 + g : 11 + g, :] = mean[10 + g : 11 + g] + kappa * moved


def gather(tables, table, member):
    tent_dev = tables[0].shape[1]
    for slot in range(SLOTS):
        table[:, slot * tent_dev : (slot + 1) * tent_dev] = tables[slot]
    high, low = split(table[...])
    found = jnp.dot(
        jnp.concatenate([high, low], axis=0), member, preferred_element_type=F32
    )
    count = table.shape[0]
    return found[:count] + found[count:]


def heights_kernel(shape, me, tents, *rest):
    *messages, out, table = rest
    for level in range(tents.shape[0]):
        member = members(tents[level : level + 1, :], me[0], shape)
        found = gather([m[32:48, :] for m in messages], table, member)
        out[level : level + 1, :] = found[9 + level : 10 + level]


def lift_weights(coef, height, means, aux, kappas):
    kappa0 = kappas[0:1, :]
    kappa1 = kappas[1:2, :]
    fields = coef.shape[0]
    first = [means[f : f + 1] - aux[f : f + 1, :] for f in range(fields)]
    second = [
        means[5 + f : 6 + f] - aux[5 + f : 6 + f, :] - kappa0 * first[f] for f in range(fields)
    ]
    moved_first = mix(coef, first)
    moved_second = mix(coef, second)
    moved_twice = mix(coef, moved_first)
    half = height * height / 2.0
    sixth = height * height * height / 6.0
    weights = []
    for f in range(fields):
        third = (
            means[10 + f : 11 + f]
            - aux[10 + f : 11 + f, :]
            - kappa1 * moved_first[f]
            - kappa0 * second[f]
        )
        weights.append(
            (
                height * first[f] + half * second[f] + sixth * third,
                half * moved_first[f] + sixth * moved_second[f],
                sixth * moved_twice[f],
            )
        )
    return weights


def element_kernel(shape, level, count, me, tents, coef, heights, kappas, old_aux, proj, *rest):
    tables = rest[:SLOTS]
    weights_out, proj_out, aux, *messages = rest[SLOTS:-2]
    vals, table = rest[-2:]
    fields = coef.shape[0]
    member = members(tents[level : level + 1, :], me[0], shape)
    means = gather([t[...] for t in tables], table, member)
    height = heights[level : level + 1, :]
    weights = lift_weights(coef, height, means, old_aux, kappas)
    weights_out[...] = jnp.zeros_like(weights_out)
    for f in range(fields):
        for k in range(3):
            weights_out[f, k : k + 1, :] = weights[f][k]
    state = mix(coef, [proj[f, 3 : 3 + count, :] for f in range(fields)])
    state = [proj[f, 2 : 2 + count, :] + height / 3.0 * state[f] for f in range(fields)]
    state = mix(coef, state)
    state = [proj[f, 1 : 1 + count, :] + height / 2.0 * state[f] for f in range(fields)]
    state = mix(coef, state)
    fresh = []
    for f in range(fields):
        value = proj[f, 0:count, :] + height * state[f]
        for k in range(3):
            value = value + kappas[k : k + count, :] * weights[f][k]
        fresh.append(value)
        proj_out[f, 0:count, :] = value
    following = members(tents[level + 1 : level + 2, :], me[0], shape)
    tent_sums(coef, following, [v[0:3] for v in fresh], aux, vals, messages, None, kappas[1:2, :])


def level_kernel(level, offset, state, coef, heights, stack, out, packed, powers):
    fields, basis, width = out.shape
    half = packed.shape[0] // 2
    base = offset if state.shape[2] > width else 0
    packed[...] = jnp.zeros_like(packed)
    for f in range(fields):
        high, low = split(state[f, :, base : base + width])
        packed[0:basis, :] = high
        packed[half : half + basis, :] = low
        product = jnp.dot(stack[...], packed[...], preferred_element_type=F32)
        powers[f] = product[: 3 * half] + product[3 * half :]

    def lanes(tile, carry):
        near = pl.multiple_of(tile * 128, 128)
        at = pl.multiple_of(offset + near, 128)
        place = pl.multiple_of(base + near, 128)
        height = heights[level : level + 1, pl.ds(at, 128)]
        factor = [
            [
                jnp.broadcast_to(height * coef[g, f : f + 1, pl.ds(at, 128)], (8, 128))
                for f in range(fields)
            ]
            for g in range(fields)
        ]

        def combine(start, values):
            mixed = []
            for g in range(fields):
                total = start[g]
                for f in range(fields):
                    total = total + factor[g][f] * values[f]
                mixed.append(total)
            return mixed

        def lines(group, inner):
            top = pl.multiple_of(group * 8, 8)

            def power(k):
                return [
                    powers[f, pl.ds(k * half + top, 8), pl.ds(near, 128)] for f in range(fields)
                ]

            value = combine(power(1), power(2))
            value = combine(power(0), value)
            start = [state[f, pl.ds(top, 8), pl.ds(place, 128)] for f in range(fields)]
            value = combine(start, value)
            for f in range(fields):
                out[f, pl.ds(top, 8), pl.ds(near, 128)] = value[f]
            return inner

        return lax.fori_loop(0, basis // 8, lines, carry, unroll=3)

    lax.fori_loop(0, width // 128, lanes, 0)


def advance(coef, height, held, count):
    fields = coef.shape[0]
    value = mix(coef, [held[f, 5 : 5 + count, :] for f in range(fields)])
    value = [held[f, 6 : 6 + count, :] + height / 3.0 * value[f] for f in range(fields)]
    value = mix(coef, value)
    value = [held[f, 7 : 7 + count, :] + height / 2.0 * value[f] for f in range(fields)]
    value = mix(coef, value)
    return [held[f, 8 : 8 + count, :] + height * value[f] for f in range(fields)]


def lift_kernel(coef, heights, weights0, weights1, lcols, *rest):
    *blocks, out, held = rest
    fields, _, n_elem = out.shape
    width = n_elem // len(blocks)
    held[...] = jnp.zeros_like(held)
    for f in range(fields):
        held[f, 8:11, :] = weights0[f, 0:3, :]
    value = advance(coef, heights[1:2, :], held, 6)
    for f in range(fields):
        held[f, 8:14, :] = value[f]
        held[f, 8:11, :] = held[f, 8:11, :] + weights1[f, 0:3, :]
    value = advance(coef, heights[2:3, :], held, 9)
    high, low = split(lcols[...])
    left = jnp.concatenate([high, high, low], axis=1)
    for f in range(fields):
        held[f, 8:17, :] = value[f]
        right_high, right_low = split(held[f, 8:24, :])
        right = jnp.concatenate([right_high, right_low, right_high], axis=0)
        added = jnp.dot(left, right, preferred_element_type=F32)
        for k, block in enumerate(blocks):
            at = slice(k * width, (k + 1) * width)
            out[f, :, at] = block[f] + added[:, at]


def closing_kernel(shape, level, me, tents, coef, heights, kappas, old_aux, lcols, state, *rest):
    tables = rest[:SLOTS]
    out, table, held, sems = rest[SLOTS:]
    fields, basis, n_elem = state.shape
    member = members(tents[level : level + 1, :], me[0], shape)
    means = gather([t[...] for t in tables], table, member)
    height = heights[level : level + 1, :]
    weights = lift_weights(coef, height, means, old_aux, kappas)
    wide = [jnp.broadcast_to(lcols[:, k : k + 1], (basis, 128)) for k in range(3)]
    copies = []
    for f in range(fields):
        for lane in range(n_elem // 128):
            at = slice(lane * 128, (lane + 1) * 128)
            value = state[f, :, at]
            for k in range(3):
                value = value + wide[k] * weights[f][k][:, at]
            held[f, :, at] = value
        copies.append(pltpu.make_async_copy(held.at[f], out.at[f], sems.at[f]))
        copies[-1].start()
    for copy in copies:
        copy.wait()


def call(kernel, outs, args, scratch=(), scalars=0, flops=1000000, space=pltpu.VMEM, out_space=pltpu.VMEM, limit=40):
    specs = [
        pl.BlockSpec(memory_space=pltpu.SMEM if i < scalars else space)
        for i in range(len(args))
    ]
    single = not isinstance(outs, (list, tuple))
    shapes = [outs] if single else list(outs)
    moved = sum(4 * s.size for s in shapes) + sum(4 * a.size for a in args)
    result = pl.pallas_call(
        kernel,
        out_shape=shapes,
        in_specs=specs,
        out_specs=[pl.BlockSpec(memory_space=out_space)] * len(shapes),
        scratch_shapes=list(scratch),
        cost_estimate=pl.CostEstimate(flops=flops, bytes_accessed=moved, transcendentals=0),
        compiler_params=pltpu.CompilerParams(vmem_limit_bytes=min(limit * 1024 * 1024, 67043328)),
    )(*args)
    return result[0] if single else result


def shaped(*dims, dtype=F32):
    return jax.ShapeDtypeStruct(dims, dtype)


def swap(x, axis, odd):
    size = lax.axis_size(axis)
    pairs = []
    for i in range(size):
        mate = (i - 1 + 2 * (i % 2)) % size if odd else i + 1 - 2 * (i % 2)
        pairs.append((i, mate))
    return lax.ppermute(x, axis, pairs)


ROUTES = ((1, "gx", True), (0, "gx", False), (3, "gy", True), (2, "gy", False))


def exchange(pieces):
    received = [None] * 4
    for slot, axis, odd in ROUTES:
        received[slot] = swap(pieces[slot], axis, odd)
    return received


def slab(state, coef, basis_quad, test_deriv, trace_vec, lift_vec, tent_height, elem_tent):
    size_first = lax.axis_size("gx")
    size_second = lax.axis_size("gy")
    fields, basis, n_elem = state.shape
    levels, tent_dev = tent_height.shape
    shape = (size_first, size_second, tent_dev)
    me = (lax.axis_index("gx") * size_second + lax.axis_index("gy")).reshape(1)
    message = [shaped(ROWS, tent_dev)] * SLOTS
    aux_shape = shaped(BACK, n_elem)
    vals = pltpu.VMEM((ROWS, n_elem), F32)
    table = pltpu.VMEM((BACK, SLOTS * tent_dev), F32)

    smat, rows3, lift, aux, *out = call(
        functools.partial(opening_kernel, shape),
        [shaped(basis, basis), shaped(8, basis), shaped(1, basis), aux_shape] + message,
        (
            me,
            *(
                pltpu.with_memory_space_constraint(x, pltpu.HBM)
                for x in (
                    basis_quad,
                    test_deriv.T,
                    trace_vec,
                    lift_vec,
                    state,
                    coef,
                    tent_height,
                    elem_tent,
                )
            ),
        ),
        [
            vals,
            pltpu.VMEM(basis_quad.shape, F32),
            pltpu.VMEM(test_deriv.shape[::-1], F32),
            pltpu.VMEM(trace_vec.shape, F32),
            pltpu.VMEM(lift_vec.shape, F32),
            pltpu.VMEM(state.shape, F32),
            pltpu.VMEM(coef.shape, F32),
            pltpu.VMEM(tent_height.shape, F32),
            pltpu.VMEM(elem_tent.shape, jnp.int32),
            pltpu.SemaphoreType.DMA((8,)),
        ],
        1,
        space=pltpu.HBM,
    )
    stack, lcols, kappas, proj = call(
        powers_kernel,
        [
            shaped(768, 256, dtype=BF16),
            shaped(basis, 16),
            shaped(16, n_elem),
            shaped(fields, 16, n_elem),
        ],
        (smat, rows3, lift, state),
        [pltpu.VMEM((16, basis), F32), pltpu.VMEM((16, basis), F32)],
        flops=100000000,
    )
    blocks = [state] * HALVES
    width = n_elem // HALVES
    weights = []
    heights = None

    def advance_block(level, half):
        blocks[half] = call(
            functools.partial(level_kernel, level, half * width),
            shaped(fields, basis, width),
            (blocks[half], coef, heights, stack),
            [pltpu.VMEM((256, width), BF16), pltpu.VMEM((fields, 384, width), F32)],
            flops=1000000000,
        )

    for level in range(levels):
        received = exchange(out[:4])
        means = call(owner_kernel, shaped(BACK, tent_dev), (kappas, out[4], *received))
        back = exchange([means] * 4)
        if level == 0:
            heights = call(
                functools.partial(heights_kernel, shape),
                shaped(8, n_elem),
                (me, elem_tent, *received, out[4]),
                [table],
                1,
                flops=10000000,
            )
        for half in range(HALVES):
            advance_block(level, half)
        if level < levels - 1:
            weight, proj, aux, *out = call(
                functools.partial(element_kernel, shape, level, 6 - 3 * level),
                [shaped(fields, 8, n_elem), shaped(fields, 8, n_elem), aux_shape] + message,
                (me, elem_tent, coef, heights, kappas, aux, proj, *back, means),
                [vals, table],
                1,
            )
            weights.append(weight)
    values = call(
        lift_kernel,
        shaped(fields, basis, n_elem),
        (coef, heights, weights[0], weights[1], lcols, *blocks),
        [pltpu.VMEM((fields, 24, n_elem), F32)],
        flops=100000000,
    )
    return call(
        functools.partial(closing_kernel, shape, levels - 1),
        shaped(fields, basis, n_elem),
        (me, elem_tent, coef, heights, kappas, aux, lcols, values, *back, means),
        [table, pltpu.VMEM(state.shape, F32), pltpu.SemaphoreType.DMA((fields,))],
        1,
        out_space=pltpu.HBM,
    )


def solution(mesh):
    placed = (
        P(None, None, ("gx", "gy")),
        P(None, None, ("gx", "gy")),
        P(),
        P(),
        P(),
        P(),
        P(None, ("gx", "gy")),
        P(None, ("gx", "gy")),
    )
    return jax.shard_map(
        slab,
        mesh=mesh,
        in_specs=placed,
        out_specs=P(None, None, ("gx", "gy")),
        check_vma=False,
    )
```

```python
import functools

import jax
import jax.numpy as jnp
from jax import lax
from jax.experimental import pallas as pl
from jax.experimental.pallas import tpu as pltpu
from jax.sharding import PartitionSpec as P


F32 = jnp.float32
BF16 = jnp.bfloat16
HIGHEST = lax.Precision.HIGHEST
ROWS = 48
BACK = 16
SLOTS = 5
HALVES = 2


def split(x):
    high = x.astype(BF16)
    return high, (x - high.astype(F32)).astype(BF16)


def exact_dot(left, right):
    return jnp.dot(left, right, precision=HIGHEST, preferred_element_type=F32)


def dot_rows(left, right):
    return lax.dot_general(
        left, right, (((1,), (1,)), ((), ())), precision=HIGHEST, preferred_element_type=F32
    )


def partners(index, size):
    even = index + 1 - 2 * lax.rem(index, 2)
    odd = lax.rem(index - 1 + 2 * lax.rem(index, 2) + size, size)
    return even, odd


def tent_columns(tents, me, size_first, size_second, tent_dev):
    first = lax.div(me, size_second)
    second = lax.rem(me, size_second)
    first_even, first_odd = partners(first, size_first)
    second_even, second_odd = partners(second, size_second)
    owners = [
        first_even * size_second + second,
        first_odd * size_second + second,
        first * size_second + second_even,
        first * size_second + second_odd,
    ]
    column = tents - (me - 4) * tent_dev
    for slot, owner in enumerate(owners):
        inside = (tents >= owner * tent_dev) & (tents < (owner + 1) * tent_dev)
        column = jnp.where(inside, tents - (owner - slot) * tent_dev, column)
    return column


def members(tents, me, shape):
    size_first, size_second, tent_dev = shape
    column = tent_columns(tents, me, size_first, size_second, tent_dev)
    full = (SLOTS * tent_dev, column.shape[1])
    lines = lax.broadcasted_iota(jnp.int32, full, 0)
    return jnp.where(lines == column, 1.0, 0.0).astype(BF16)


def mix(coef, values):
    mixed = []
    for target in range(len(values)):
        total = coef[target, 0:1, :] * values[0]
        for source in range(1, len(values)):
            total = total + coef[target, source : source + 1, :] * values[source]
        mixed.append(total)
    return mixed


def tent_sums(coef, member, traces, aux, vals, messages, heights, kappa):
    fields = len(traces)
    once = mix(coef, traces)
    twice = mix(coef, once)
    vals[...] = jnp.zeros_like(vals)
    aux[...] = jnp.zeros_like(aux)
    for f in range(fields):
        vals[f : f + 1, :] = traces[f][0:1]
        vals[5 + f : 6 + f, :] = once[f][1:2]
        vals[10 + f : 11 + f, :] = twice[f][2:3] - kappa * once[f][0:1]
        vals[15 + 5 * f : 20 + 5 * f, :] = coef[f]
        aux[f : f + 1, :] = traces[f][0:1]
        aux[5 + f : 6 + f, :] = once[f][1:2]
        aux[10 + f : 11 + f, :] = twice[f][2:3]
    vals[40:41, :] = jnp.ones_like(vals[40:41, :])
    high, low = split(vals[...])
    both = jnp.concatenate([high, low], axis=0)
    sums = lax.dot_general(
        both, member, (((1,), (1,)), ((), ())), preferred_element_type=F32
    )
    sums = sums[:ROWS] + sums[ROWS:]
    tent_dev = messages[0].shape[1]
    for slot in range(SLOTS):
        messages[slot][...] = sums[:, slot * tent_dev : (slot + 1) * tent_dev]
        if heights is not None:
            messages[slot][41:44, :] = heights[...]


def opening_kernel(shape, me, basis_in, test_in, trace_in, lift_in, state_in, coef_in, *rest):
    heights_in, tents_in, rows3, lift_row, aux, *rest = rest
    messages = rest[:SLOTS]
    vals, basis, test, trace, lift, state, coef, heights, tents, wide, found, sems = rest[SLOTS:]
    sources = (test_in, trace_in, basis_in, lift_in, tents_in, state_in, coef_in, heights_in)
    targets = (test, trace, basis, lift, tents, state, coef, heights)
    copies = [
        pltpu.make_async_copy(source, target, sems.at[k])
        for k, (source, target) in enumerate(zip(sources, targets))
    ]
    for copy in copies:
        copy.start()
    count = trace.shape[0]
    copies[4].wait()
    member = members(tents[0:1, :], me[0], shape)
    for k in range(4):
        copies[k].wait()
    row = trace[...].reshape(1, count)
    rows3[...] = jnp.zeros_like(rows3)
    rows3[0:1, :] = row
    for k in (1, 2):
        tested = jnp.sum(test[...] * row, axis=1, keepdims=True)
        row = jnp.sum(basis[...] * tested, axis=0, keepdims=True)
        rows3[k : k + 1, :] = row
    lift_row[...] = lift[...].reshape(1, count)
    kappa = jnp.sum(rows3[1:2, :] * lift_row[...], axis=1, keepdims=True)
    columns = rows3[...].T
    for k in range(3):
        wide[k] = jnp.broadcast_to(columns[:, k : k + 1], (count, 128))
    copies[5].wait()
    fields = state.shape[0]
    for pair in range(state.shape[2] // 256):
        lanes = [slice(pair * 256 + part * 128, pair * 256 + part * 128 + 128) for part in range(2)]
        totals = {}
        for group in range(count // 8):
            lines = slice(group * 8, group * 8 + 8)
            vector = [wide[k, lines, :] for k in range(3)]
            for f in range(fields):
                for part in range(2):
                    block = state[f, lines, lanes[part]]
                    for k in range(3):
                        term = block * vector[k]
                        held = totals.get((f, part, k))
                        totals[f, part, k] = term if held is None else held + term
        for (f, part, k), total in totals.items():
            found[f, k : k + 1, lanes[part]] = jnp.sum(total, axis=0, keepdims=True)
    copies[6].wait()
    copies[7].wait()
    traces = [found[f, 0:3, :] for f in range(fields)]
    tent_sums(coef, member, traces, aux, vals, messages, heights, kappa)


def powers_kernel(basis, test, rows3, lift, stack, rstack, lcols, kappas, rows, lrows):
    s1 = lax.dot_general(
        test[...],
        basis[...],
        (((0,), (0,)), ((), ())),
        precision=HIGHEST,
        preferred_element_type=F32,
    )
    count = s1.shape[0]
    s2 = exact_dot(s1, s1)
    s3 = exact_dot(s2, s1)
    s4 = exact_dot(s2, s2)
    stack[...] = jnp.zeros_like(stack)
    rstack[...] = jnp.zeros_like(rstack)
    half = stack.shape[1] // 2
    rows[...] = jnp.zeros_like(rows)
    lrows[...] = jnp.zeros_like(lrows)
    rows[0:2, :] = rows3[0:2, :]
    rows[2:4, :] = exact_dot(rows3[0:2, :], s2)
    rows[4:8, :] = exact_dot(rows[0:4, :], s4)
    rows[8:9, :] = exact_dot(rows[4:5, :], s4)
    lrows[0:1, :] = lift[...]
    lrows[1:2, :] = dot_rows(lift[...], s1)
    lrows[2:4, :] = dot_rows(lrows[0:2, :], s2)
    lrows[4:8, :] = dot_rows(lrows[0:4, :], s4)
    lrows[8:9, :] = dot_rows(lrows[4:5, :], s4)
    lcols[...] = lrows[...].T
    kappas[...] = jnp.broadcast_to(
        jnp.sum(rows[...] * lift[...], axis=1, keepdims=True), kappas.shape
    )
    row_high, row_low = split(rows[...])
    for side in range(2):
        columns = slice(side * half, side * half + count)
        for power, matrix in enumerate((s1, s2 / 2.0, s3 / 6.0)):
            high, low = split(matrix)
            stack[power * half : power * half + count, columns] = high
            stack[(3 + power) * half : (3 + power) * half + count, columns] = low
        rstack[0:16, columns] = row_high
        rstack[16:32, columns] = row_low


def projections_kernel(rstack, state, out, packed):
    fields, count, n_elem = state.shape
    width = packed.shape[1]
    half = packed.shape[0] // 2
    packed[...] = jnp.zeros_like(packed)
    for f in range(fields):
        for block in range(n_elem // width):
            at = slice(block * width, (block + 1) * width)
            high, low = split(state[f, :, at])
            packed[0:count, :] = high
            packed[half : half + count, :] = low
            product = jnp.dot(rstack[...], packed[...], preferred_element_type=F32)
            out[f, :, at] = product[:16] + product[16:]


def owner_kernel(kappas, own, *rest):
    *received, out = rest
    total = own[...]
    for ref in received:
        total = total + ref[...]
    mean = total / jnp.maximum(total[40:41], 1.0)
    first = mean[0:5]
    out[...] = jnp.zeros_like(out)
    out[0:10, :] = mean[0:10]
    kappa = kappas[1:2, 0 : out.shape[1]]
    for g in range(5):
        moved = jnp.sum(mean[15 + 5 * g : 20 + 5 * g] * first, axis=0, keepdims=True)
        out[10 + g : 11 + g, :] = mean[10 + g : 11 + g] + kappa * moved


def gather(tables, table, member):
    tent_dev = tables[0].shape[1]
    for slot in range(SLOTS):
        table[:, slot * tent_dev : (slot + 1) * tent_dev] = tables[slot]
    high, low = split(table[...])
    found = jnp.dot(
        jnp.concatenate([high, low], axis=0), member, preferred_element_type=F32
    )
    count = table.shape[0]
    return found[:count] + found[count:]


def heights_kernel(shape, me, tents, *rest):
    *messages, out, table = rest
    for level in range(tents.shape[0]):
        member = members(tents[level : level + 1, :], me[0], shape)
        found = gather([m[32:48, :] for m in messages], table, member)
        out[level : level + 1, :] = found[9 + level : 10 + level]


def lift_weights(coef, height, means, aux, kappas):
    kappa0 = kappas[0:1, :]
    kappa1 = kappas[1:2, :]
    fields = coef.shape[0]
    first = [means[f : f + 1] - aux[f : f + 1, :] for f in range(fields)]
    second = [
        means[5 + f : 6 + f] - aux[5 + f : 6 + f, :] - kappa0 * first[f] for f in range(fields)
    ]
    moved_first = mix(coef, first)
    moved_second = mix(coef, second)
    moved_twice = mix(coef, moved_first)
    half = height * height / 2.0
    sixth = height * height * height / 6.0
    weights = []
    for f in range(fields):
        third = (
            means[10 + f : 11 + f]
            - aux[10 + f : 11 + f, :]
            - kappa1 * moved_first[f]
            - kappa0 * second[f]
        )
        weights.append(
            (
                height * first[f] + half * second[f] + sixth * third,
                half * moved_first[f] + sixth * moved_second[f],
                sixth * moved_twice[f],
            )
        )
    return weights


def element_kernel(shape, level, count, me, tents, coef, heights, kappas, old_aux, proj, *rest):
    tables = rest[:SLOTS]
    weights_out, aux, *messages = rest[SLOTS : 2 * SLOTS + 2]
    proj_out = rest[2 * SLOTS + 2] if count > 3 else None
    vals, table = rest[-2:]
    fields = coef.shape[0]
    member = members(tents[level : level + 1, :], me[0], shape)
    means = gather([t[...] for t in tables], table, member)
    height = heights[level : level + 1, :]
    weights = lift_weights(coef, height, means, old_aux, kappas)
    weights_out[...] = jnp.zeros_like(weights_out)
    for f in range(fields):
        for k in range(3):
            weights_out[f, k : k + 1, :] = weights[f][k]
    state = mix(coef, [proj[f, 3 : 3 + count, :] for f in range(fields)])
    state = [proj[f, 2 : 2 + count, :] + height / 3.0 * state[f] for f in range(fields)]
    state = mix(coef, state)
    state = [proj[f, 1 : 1 + count, :] + height / 2.0 * state[f] for f in range(fields)]
    state = mix(coef, state)
    fresh = []
    for f in range(fields):
        value = proj[f, 0:count, :] + height * state[f]
        for k in range(3):
            value = value + kappas[k : k + count, :] * weights[f][k]
        fresh.append(value)
        if proj_out is not None:
            proj_out[f, 0:count, :] = value
    following = members(tents[level + 1 : level + 2, :], me[0], shape)
    tent_sums(coef, following, [v[0:3] for v in fresh], aux, vals, messages, None, kappas[1:2, :])


def level_kernel(level, offset, state, coef, heights, stack, out, packed, powers):
    fields, basis, width = out.shape
    half = packed.shape[0] // 2
    base = offset if state.shape[2] > width else 0
    packed[...] = jnp.zeros_like(packed)
    for f in range(fields):
        high, low = split(state[f, :, base : base + width])
        packed[0:basis, :] = high
        packed[half : half + basis, :] = low
        product = jnp.dot(stack[...], packed[...], preferred_element_type=F32)
        powers[f] = product[: 3 * half] + product[3 * half :]

    def lanes(tile, carry):
        near = pl.multiple_of(tile * 128, 128)
        at = pl.multiple_of(offset + near, 128)
        place = pl.multiple_of(base + near, 128)
        height = heights[level : level + 1, pl.ds(at, 128)]
        factor = [
            [
                jnp.broadcast_to(height * coef[g, f : f + 1, pl.ds(at, 128)], (8, 128))
                for f in range(fields)
            ]
            for g in range(fields)
        ]

        def combine(start, values):
            mixed = []
            for g in range(fields):
                total = start[g]
                for f in range(fields):
                    total = total + factor[g][f] * values[f]
                mixed.append(total)
            return mixed

        def lines(group, inner):
            top = pl.multiple_of(group * 8, 8)

            def power(k):
                return [
                    powers[f, pl.ds(k * half + top, 8), pl.ds(near, 128)] for f in range(fields)
                ]

            value = combine(power(1), power(2))
            value = combine(power(0), value)
            start = [state[f, pl.ds(top, 8), pl.ds(place, 128)] for f in range(fields)]
            value = combine(start, value)
            for f in range(fields):
                out[f, pl.ds(top, 8), pl.ds(near, 128)] = value[f]
            return inner

        return lax.fori_loop(0, basis // 8, lines, carry, unroll=3)

    lax.fori_loop(0, width // 128, lanes, 0)


def advance(coef, height, held, count):
    fields = coef.shape[0]
    value = mix(coef, [held[f, 5 : 5 + count, :] for f in range(fields)])
    value = [held[f, 6 : 6 + count, :] + height / 3.0 * value[f] for f in range(fields)]
    value = mix(coef, value)
    value = [held[f, 7 : 7 + count, :] + height / 2.0 * value[f] for f in range(fields)]
    value = mix(coef, value)
    return [held[f, 8 : 8 + count, :] + height * value[f] for f in range(fields)]


def lift_kernel(coef, heights, weights0, weights1, lcols, *rest):
    *blocks, out, held = rest
    fields, _, n_elem = out.shape
    width = n_elem // len(blocks)
    held[...] = jnp.zeros_like(held)
    for f in range(fields):
        held[f, 8:11, :] = weights0[f, 0:3, :]
    value = advance(coef, heights[1:2, :], held, 6)
    for f in range(fields):
        held[f, 8:14, :] = value[f]
        held[f, 8:11, :] = held[f, 8:11, :] + weights1[f, 0:3, :]
    value = advance(coef, heights[2:3, :], held, 9)
    high, low = split(lcols[...])
    left = jnp.concatenate([high, high, low], axis=1)
    for f in range(fields):
        held[f, 8:17, :] = value[f]
        right_high, right_low = split(held[f, 8:24, :])
        right = jnp.concatenate([right_high, right_low, right_high], axis=0)
        added = jnp.dot(left, right, preferred_element_type=F32)
        for k, block in enumerate(blocks):
            at = slice(k * width, (k + 1) * width)
            out[f, :, at] = block[f] + added[:, at]


def closing_kernel(shape, level, me, tents, coef, heights, kappas, old_aux, lcols, state, *rest):
    tables = rest[:SLOTS]
    out, table, held, wide, sems = rest[SLOTS:]
    fields, basis, n_elem = state.shape
    member = members(tents[level : level + 1, :], me[0], shape)
    means = gather([t[...] for t in tables], table, member)
    height = heights[level : level + 1, :]
    weights = lift_weights(coef, height, means, old_aux, kappas)
    for k in range(3):
        wide[k] = jnp.broadcast_to(lcols[:, k : k + 1], (basis, 128))
    copies = []
    for f in range(fields):
        for pair in range(n_elem // 256):
            lanes = [
                slice(pair * 256 + part * 128, pair * 256 + part * 128 + 128) for part in range(2)
            ]
            scale = [
                [jnp.broadcast_to(weights[f][k][:, at], (8, 128)) for k in range(3)]
                for at in lanes
            ]
            for group in range(basis // 8):
                lines = slice(group * 8, group * 8 + 8)
                vector = [wide[k, lines, :] for k in range(3)]
                for part in range(2):
                    value = state[f, lines, lanes[part]]
                    for k in range(3):
                        value = value + vector[k] * scale[part][k]
                    held[f, lines, lanes[part]] = value
        copies.append(pltpu.make_async_copy(held.at[f], out.at[f], sems.at[f]))
        copies[-1].start()
    for copy in copies:
        copy.wait()


def call(kernel, outs, args, scratch=(), scalars=0, flops=1000000, space=pltpu.VMEM, out_space=pltpu.VMEM, limit=40):
    specs = [
        pl.BlockSpec(memory_space=pltpu.SMEM if i < scalars else space)
        for i in range(len(args))
    ]
    single = not isinstance(outs, (list, tuple))
    shapes = [outs] if single else list(outs)
    moved = sum(4 * s.size for s in shapes) + sum(4 * a.size for a in args)
    result = pl.pallas_call(
        kernel,
        out_shape=shapes,
        in_specs=specs,
        out_specs=[pl.BlockSpec(memory_space=out_space)] * len(shapes),
        scratch_shapes=list(scratch),
        cost_estimate=pl.CostEstimate(flops=flops, bytes_accessed=moved, transcendentals=0),
        compiler_params=pltpu.CompilerParams(vmem_limit_bytes=min(limit * 1024 * 1024, 67043328)),
    )(*args)
    return result[0] if single else result


def shaped(*dims, dtype=F32):
    return jax.ShapeDtypeStruct(dims, dtype)


def swap(x, axis, odd):
    size = lax.axis_size(axis)
    pairs = []
    for i in range(size):
        mate = (i - 1 + 2 * (i % 2)) % size if odd else i + 1 - 2 * (i % 2)
        pairs.append((i, mate))
    return lax.ppermute(x, axis, pairs)


ROUTES = ((1, "gx", True), (0, "gx", False), (3, "gy", True), (2, "gy", False))


def exchange(pieces):
    received = [None] * 4
    for slot, axis, odd in ROUTES:
        received[slot] = swap(pieces[slot], axis, odd)
    return received


def slab(state, coef, basis_quad, test_deriv, trace_vec, lift_vec, tent_height, elem_tent):
    size_first = lax.axis_size("gx")
    size_second = lax.axis_size("gy")
    fields, basis, n_elem = state.shape
    levels, tent_dev = tent_height.shape
    shape = (size_first, size_second, tent_dev)
    me = (lax.axis_index("gx") * size_second + lax.axis_index("gy")).reshape(1)
    message = [shaped(ROWS, tent_dev)] * SLOTS
    aux_shape = shaped(BACK, n_elem)
    vals = pltpu.VMEM((ROWS, n_elem), F32)
    table = pltpu.VMEM((BACK, SLOTS * tent_dev), F32)

    rows3, lift, aux, *out = call(
        functools.partial(opening_kernel, shape),
        [shaped(8, basis), shaped(1, basis), aux_shape] + message,
        (
            me,
            *(
                pltpu.with_memory_space_constraint(x, pltpu.HBM)
                for x in (
                    basis_quad,
                    test_deriv.T,
                    trace_vec,
                    lift_vec,
                    state,
                    coef,
                    tent_height,
                    elem_tent,
                )
            ),
        ),
        [
            vals,
            pltpu.VMEM(basis_quad.shape, F32),
            pltpu.VMEM(test_deriv.shape[::-1], F32),
            pltpu.VMEM(trace_vec.shape, F32),
            pltpu.VMEM(lift_vec.shape, F32),
            pltpu.VMEM(state.shape, F32),
            pltpu.VMEM(coef.shape, F32),
            pltpu.VMEM(tent_height.shape, F32),
            pltpu.VMEM(elem_tent.shape, jnp.int32),
            pltpu.VMEM((3, basis, 128), F32),
            pltpu.VMEM((fields, 8, n_elem), F32),
            pltpu.SemaphoreType.DMA((8,)),
        ],
        1,
        space=pltpu.HBM,
    )
    stack, rstack, lcols, kappas = call(
        powers_kernel,
        [
            shaped(768, 256, dtype=BF16),
            shaped(32, 256, dtype=BF16),
            shaped(basis, 16),
            shaped(16, n_elem),
        ],
        (basis_quad, test_deriv.T, rows3, lift),
        [pltpu.VMEM((16, basis), F32), pltpu.VMEM((16, basis), F32)],
        flops=100000000,
    )
    proj = call(
        projections_kernel,
        shaped(fields, 16, n_elem),
        (rstack, state),
        [pltpu.VMEM((256, 256), BF16)],
        flops=300000000,
    )
    blocks = [state] * HALVES
    width = n_elem // HALVES
    weights = []
    heights = None

    def advance_block(level, half):
        blocks[half] = call(
            functools.partial(level_kernel, level, half * width),
            shaped(fields, basis, width),
            (blocks[half], coef, heights, stack),
            [pltpu.VMEM((256, width), BF16), pltpu.VMEM((fields, 384, width), F32)],
            flops=1000000000,
        )

    for level in range(levels):
        received = exchange(out[:4])
        means = call(owner_kernel, shaped(BACK, tent_dev), (kappas, out[4], *received))
        back = exchange([means] * 4)
        if level == 0:
            heights = call(
                functools.partial(heights_kernel, shape),
                shaped(8, n_elem),
                (me, elem_tent, *received, out[4]),
                [table],
                1,
                flops=10000000,
            )
        for half in range(HALVES):
            advance_block(level, half)
        if level < levels - 1:
            more = [shaped(fields, 8, n_elem)] if level < levels - 2 else []
            weight, aux, *out = call(
                functools.partial(element_kernel, shape, level, 6 - 3 * level),
                [shaped(fields, 8, n_elem), aux_shape] + message + more,
                (me, elem_tent, coef, heights, kappas, aux, proj, *back, means),
                [vals, table],
                1,
            )
            weights.append(weight)
            if more:
                proj = out.pop()
    values = call(
        lift_kernel,
        shaped(fields, basis, n_elem),
        (coef, heights, weights[0], weights[1], lcols, *blocks),
        [pltpu.VMEM((fields, 24, n_elem), F32)],
        flops=100000000,
    )
    return call(
        functools.partial(closing_kernel, shape, levels - 1),
        shaped(fields, basis, n_elem),
        (me, elem_tent, coef, heights, kappas, aux, lcols, values, *back, means),
        [
            table,
            pltpu.VMEM(state.shape, F32),
            pltpu.VMEM((3, basis, 128), F32),
            pltpu.SemaphoreType.DMA((fields,)),
        ],
        1,
        out_space=pltpu.HBM,
    )


def solution(mesh):
    placed = (
        P(None, None, ("gx", "gy")),
        P(None, None, ("gx", "gy")),
        P(),
        P(),
        P(),
        P(),
        P(None, ("gx", "gy")),
        P(None, ("gx", "gy")),
    )
    return jax.shard_map(
        slab,
        mesh=mesh,
        in_specs=placed,
        out_specs=P(None, None, ("gx", "gy")),
        check_vma=False,
    )
```

```python
import functools

import jax
import jax.numpy as jnp
from jax import lax
from jax.experimental import pallas as pl
from jax.experimental.pallas import tpu as pltpu
from jax.sharding import PartitionSpec as P


F32 = jnp.float32
BF16 = jnp.bfloat16
HIGHEST = lax.Precision.HIGHEST
ROWS = 48
BACK = 16
SLOTS = 5
HALVES = 2


def split(x):
    high = x.astype(BF16)
    return high, (x - high.astype(F32)).astype(BF16)


def exact_dot(left, right):
    return jnp.dot(left, right, precision=HIGHEST, preferred_element_type=F32)


def partners(index, size):
    even = index + 1 - 2 * lax.rem(index, 2)
    odd = lax.rem(index - 1 + 2 * lax.rem(index, 2) + size, size)
    return even, odd


def tent_columns(tents, me, size_first, size_second, tent_dev):
    first = lax.div(me, size_second)
    second = lax.rem(me, size_second)
    first_even, first_odd = partners(first, size_first)
    second_even, second_odd = partners(second, size_second)
    owners = [
        first_even * size_second + second,
        first_odd * size_second + second,
        first * size_second + second_even,
        first * size_second + second_odd,
    ]
    column = tents - (me - 4) * tent_dev
    for slot, owner in enumerate(owners):
        inside = (tents >= owner * tent_dev) & (tents < (owner + 1) * tent_dev)
        column = jnp.where(inside, tents - (owner - slot) * tent_dev, column)
    return column


def members(tents, me, shape):
    size_first, size_second, tent_dev = shape
    column = tent_columns(tents, me, size_first, size_second, tent_dev)
    full = (SLOTS * tent_dev, column.shape[1])
    lines = lax.broadcasted_iota(jnp.int32, full, 0)
    return jnp.where(lines == column, 1.0, 0.0).astype(BF16)


def mix(coef, values):
    mixed = []
    for target in range(len(values)):
        total = coef[target, 0:1, :] * values[0]
        for source in range(1, len(values)):
            total = total + coef[target, source : source + 1, :] * values[source]
        mixed.append(total)
    return mixed


def tent_sums(coef, member, traces, aux, vals, messages, heights, kappa):
    fields = len(traces)
    once = mix(coef, traces)
    twice = mix(coef, once)
    vals[...] = jnp.zeros_like(vals)
    aux[...] = jnp.zeros_like(aux)
    for f in range(fields):
        vals[f : f + 1, :] = traces[f][0:1]
        vals[5 + f : 6 + f, :] = once[f][1:2]
        vals[10 + f : 11 + f, :] = twice[f][2:3] - kappa * once[f][0:1]
        vals[15 + 5 * f : 20 + 5 * f, :] = coef[f]
        aux[f : f + 1, :] = traces[f][0:1]
        aux[5 + f : 6 + f, :] = once[f][1:2]
        aux[10 + f : 11 + f, :] = twice[f][2:3]
    vals[40:41, :] = jnp.ones_like(vals[40:41, :])
    high, low = split(vals[...])
    both = jnp.concatenate([high, low], axis=0)
    sums = lax.dot_general(
        both, member, (((1,), (1,)), ((), ())), preferred_element_type=F32
    )
    sums = sums[:ROWS] + sums[ROWS:]
    rows, tent_dev = messages[0].shape[0], messages[0].shape[1] // 2
    for slot in range(SLOTS):
        columns = slice(slot * tent_dev, (slot + 1) * tent_dev)
        messages[slot][:, :tent_dev] = sums[:rows, columns]
        messages[slot][:, tent_dev:] = sums[rows:, columns]
        if heights is not None:
            messages[slot][41 - rows : 44 - rows, tent_dev:] = heights[...]


def opening_kernel(shape, me, basis_in, test_in, trace_in, lift_in, state_in, coef_in, *rest):
    heights_in, tents_in, rows3, lift_row, aux, *rest = rest
    messages = rest[:SLOTS]
    basis, test, state, coef, tents, *rest = rest[SLOTS:]
    vals, trace, lift, heights, wide, found, sems = rest
    sources = (test_in, trace_in, basis_in, lift_in, tents_in, state_in, coef_in, heights_in)
    targets = (test, trace, basis, lift, tents, state, coef, heights)
    copies = [
        pltpu.make_async_copy(source, target, sems.at[k])
        for k, (source, target) in enumerate(zip(sources, targets))
    ]
    for copy in copies:
        copy.start()
    count = trace.shape[0]
    copies[4].wait()
    member = members(tents[0:1, :], me[0], shape)
    for k in range(4):
        copies[k].wait()
    row = trace[...].reshape(1, count)
    rows3[...] = jnp.zeros_like(rows3)
    rows3[0:1, :] = row
    for k in (1, 2):
        tested = jnp.sum(test[...] * row, axis=1, keepdims=True)
        row = jnp.sum(basis[...] * tested, axis=0, keepdims=True)
        rows3[k : k + 1, :] = row
    lift_row[...] = lift[...].reshape(1, count)
    kappa = jnp.sum(rows3[1:2, :] * lift_row[...], axis=1, keepdims=True)
    columns = rows3[...].T
    for k in range(3):
        wide[k] = jnp.broadcast_to(columns[:, k : k + 1], (count, 128))
    copies[5].wait()
    fields = state.shape[0]
    for pair in range(state.shape[2] // 256):
        lanes = [slice(pair * 256 + part * 128, pair * 256 + part * 128 + 128) for part in range(2)]
        totals = {}
        for group in range(count // 8):
            lines = slice(group * 8, group * 8 + 8)
            vector = [wide[k, lines, :] for k in range(3)]
            for f in range(fields):
                for part in range(2):
                    block = state[f, lines, lanes[part]]
                    for k in range(3):
                        term = block * vector[k]
                        held = totals.get((f, part, k))
                        totals[f, part, k] = term if held is None else held + term
        for (f, part, k), total in totals.items():
            found[f, k : k + 1, lanes[part]] = jnp.sum(total, axis=0, keepdims=True)
    copies[6].wait()
    copies[7].wait()
    traces = [found[f, 0:3, :] for f in range(fields)]
    tent_sums(coef, member, traces, aux, vals, messages, heights, kappa)


def powers_kernel(basis, test, rows3, lift, stack, rstack, lcols, kappas, rows, left, right):
    count = basis.shape[1]
    first, second = slice(8, 8 + count), slice(8 + count, 8 + 2 * count)
    extra = right.shape[1]
    s1 = lax.dot_general(
        test[...],
        basis[...],
        (((0,), (0,)), ((), ())),
        precision=HIGHEST,
        preferred_element_type=F32,
    )
    stack[...] = jnp.zeros_like(stack)
    rstack[...] = jnp.zeros_like(rstack)
    rows[...] = jnp.zeros_like(rows)
    left[...] = jnp.zeros_like(left)
    right[...] = jnp.zeros_like(right)
    lcols[...] = jnp.zeros_like(lcols)
    rows[8:9, :] = lift[...]
    lcols[:, 0:8] = rows[8:16, :].T
    rows[0:3, :] = rows3[0:3, :]
    left[0:8, :] = rows[0:8, :]
    left[first, :] = s1
    right[:, 0:count] = s1
    right[:, count:extra] = lcols[:, 0:8]
    product = exact_dot(left[0 : 8 + count, :], right[...])
    s2 = product[first, 0:count]
    rows[3:4, :] = product[2:3, 0:count]
    lcols[:, 1:2] = product[first, count : count + 1]
    left[0:8, :] = rows[0:8, :]
    left[second, :] = s2
    right[:, 0:count] = s2
    right[:, count:extra] = lcols[:, 0:8]
    product = exact_dot(left[0 : 8 + 2 * count, :], right[...])
    s3 = product[first, 0:count]
    s4 = product[second, 0:count]
    rows[4:6, :] = product[2:4, 0:count]
    lcols[:, 2:4] = product[second, count : count + 2]
    left[0:4, :] = rows[2:6, :]
    left[first, :] = s4
    right[:, 0:count] = s4
    right[:, count:extra] = lcols[:, 0:8]
    product = exact_dot(left[0 : 8 + count, :], right[...])
    rows[6:9, :] = product[0:3, 0:count]
    lcols[:, 4:8] = product[first, count : count + 4]
    lcols[:, 8:9] = jnp.sum(product[first, 0:count] * lift[...], axis=1, keepdims=True)
    kappas[...] = jnp.broadcast_to(
        jnp.sum(rows[...] * lift[...], axis=1, keepdims=True), kappas.shape
    )
    half = rstack.shape[1] // 2
    row_high, row_low = split(rows[...])
    for side in range(2):
        columns = slice(side * half, side * half + count)
        for power, matrix in enumerate((s1, s2 / 2.0, s3 / 6.0)):
            high, low = split(matrix)
            stack[power * half : power * half + count, columns] = high
            stack[(3 + power) * half : (3 + power) * half + count, columns] = low
        rstack[0:16, columns] = row_high
        rstack[16:32, columns] = row_low


def projections_kernel(rstack, state, out, packed):
    fields, count, n_elem = state.shape
    width = packed.shape[1]
    half = packed.shape[0] // 2
    packed[...] = jnp.zeros_like(packed)
    for f in range(fields):
        for block in range(n_elem // width):
            at = slice(block * width, (block + 1) * width)
            high, low = split(state[f, :, at])
            packed[0:count, :] = high
            packed[half : half + count, :] = low
            product = jnp.dot(rstack[...], packed[...], preferred_element_type=F32)
            out[f, :, at] = product[:16] + product[16:]


def owner_kernel(kappas, own, *rest):
    *received, out = rest
    total = own[...]
    for ref in received:
        total = total + ref[...]
    total = jnp.concatenate([total[:, : out.shape[1]], total[:, out.shape[1] :]], axis=0)
    mean = total / jnp.maximum(total[40:41], 1.0)
    first = mean[0:5]
    out[...] = jnp.zeros_like(out)
    out[0:10, :] = mean[0:10]
    kappa = kappas[1:2, 0 : out.shape[1]]
    for g in range(5):
        moved = jnp.sum(mean[15 + 5 * g : 20 + 5 * g] * first, axis=0, keepdims=True)
        out[10 + g : 11 + g, :] = mean[10 + g : 11 + g] + kappa * moved


def gather(tables, table, member):
    tent_dev = table.shape[1] // SLOTS
    for slot in range(SLOTS):
        table[:, slot * tent_dev : (slot + 1) * tent_dev] = tables[slot]
    high, low = split(table[...])
    found = jnp.dot(
        jnp.concatenate([high, low], axis=0), member, preferred_element_type=F32
    )
    count = table.shape[0]
    return found[:count] + found[count:]


def members_kernel(shape, me, tents, *outs):
    for level, out in enumerate(outs):
        out[...] = members(tents[level : level + 1, :], me[0], shape)


def heights_kernel(messages, memberships, out, table):
    out[...] = jnp.zeros_like(out)
    half = messages[0].shape[1] // 2
    for level, member in enumerate(memberships):
        found = gather([m[8:24, half:] for m in messages], table, member[...])
        out[level : level + 1, :] = found[9 + level : 10 + level]


def drift_kernel(level, count, coef, heights, proj, out):
    fields = coef.shape[0]
    height = heights[level : level + 1, :]
    state = mix(coef, [proj[f, 3 : 3 + count, :] for f in range(fields)])
    state = [proj[f, 2 : 2 + count, :] + height / 3.0 * state[f] for f in range(fields)]
    state = mix(coef, state)
    state = [proj[f, 1 : 1 + count, :] + height / 2.0 * state[f] for f in range(fields)]
    state = mix(coef, state)
    for f in range(fields):
        out[f, 0:count, :] = proj[f, 0:count, :] + height * state[f]


def lift_weights(coef, height, means, aux, kappas):
    kappa0 = kappas[0:1, :]
    kappa1 = kappas[1:2, :]
    fields = coef.shape[0]
    first = [means[f : f + 1] - aux[f : f + 1, :] for f in range(fields)]
    second = [
        means[5 + f : 6 + f] - aux[5 + f : 6 + f, :] - kappa0 * first[f] for f in range(fields)
    ]
    moved = mix(coef, [jnp.concatenate([first[f], second[f]], axis=0) for f in range(fields)])
    moved_first = [m[0:1] for m in moved]
    moved_second = [m[1:2] for m in moved]
    moved_twice = mix(coef, moved_first)
    half = height * height / 2.0
    sixth = height * height * height / 6.0
    weights = []
    for f in range(fields):
        third = (
            means[10 + f : 11 + f]
            - aux[10 + f : 11 + f, :]
            - kappa1 * moved_first[f]
            - kappa0 * second[f]
        )
        weights.append(
            (
                height * first[f] + half * second[f] + sixth * third,
                half * moved_first[f] + sixth * moved_second[f],
                sixth * moved_twice[f],
            )
        )
    return weights


def element_kernel(level, count, coef, heights, kappas, old_aux, drift, member, following, *rest):
    tables = rest[:SLOTS]
    weights_out, aux, *messages = rest[SLOTS : 2 * SLOTS + 2]
    proj_out = rest[2 * SLOTS + 2] if count > 3 else None
    vals, table = rest[-2:]
    fields = coef.shape[0]
    means = gather([t[...] for t in tables], table, member[...])
    height = heights[level : level + 1, :]
    weights = lift_weights(coef, height, means, old_aux, kappas)
    weights_out[...] = jnp.zeros_like(weights_out)
    fresh = []
    for f in range(fields):
        for k in range(3):
            weights_out[f, k : k + 1, :] = weights[f][k]
        value = drift[f, 0:count, :]
        for k in range(3):
            value = value + kappas[k : k + count, :] * weights[f][k]
        fresh.append(value)
        if proj_out is not None:
            proj_out[f, 0:count, :] = value
    tent_sums(
        coef,
        following[...],
        [v[0:3] for v in fresh],
        aux,
        vals,
        messages,
        None,
        kappas[1:2, :],
    )


def poly_kernel(steps, resumed, state, coef, heights, stack, *rest):
    rest = list(rest)
    current = rest.pop(0) if resumed else None
    moves = any(mixed is not None for mixed, _ in steps)
    out = rest.pop(0) if moves else None
    left = rest.pop(0) if steps[-1][1] is not None else None
    packed, powers, factors = rest
    fields, basis, n_elem = state.shape
    width = n_elem // HALVES
    half_rows = packed.shape[1] // 2
    written = set()
    packed[...] = jnp.zeros_like(packed)

    def multiply(f, half, target):
        source = out if half in written else state
        high, low = split(source[f, :, half * width : (half + 1) * width])
        slot = f % 2
        packed[slot, 0:basis, :] = high
        packed[slot, half_rows : half_rows + basis, :] = low
        product = jnp.dot(stack[...], packed[slot], preferred_element_type=F32)
        target[f] = product[: 3 * half_rows] + product[3 * half_rows :]

    def set_factors(level, half):
        at = slice(half * width, (half + 1) * width)
        height = heights[level : level + 1, at]
        for g in range(fields):
            for f in range(fields):
                factors[g * fields + f] = jnp.broadcast_to(
                    height * coef[g, f : f + 1, at], (8, width)
                )

    def mix_lines(half, groups, values):
        base = out if half in written else state
        for tile in range(width // 128):
            near = slice(tile * 128, (tile + 1) * 128)
            at = slice(half * width + tile * 128, half * width + (tile + 1) * 128)
            factor = [factors[k, :, near] for k in range(fields * fields)]

            def combine(start, values):
                mixed = []
                for g in range(fields):
                    total = start[g]
                    for f in range(fields):
                        total = total + factor[g * fields + f] * values[f]
                    mixed.append(total)
                return mixed

            for group in groups:
                lines = slice(group * 8, group * 8 + 8)

                def power(k):
                    rows = slice(k * half_rows + group * 8, k * half_rows + group * 8 + 8)
                    return [values[f, rows, near] for f in range(fields)]

                value = combine(power(1), power(2))
                value = combine(power(0), value)
                value = combine([base[f, lines, at] for f in range(fields)], value)
                for f in range(fields):
                    out[f, lines, at] = value[f]

    groups = basis // 8 // fields
    for index, (mixed, multiplied) in enumerate(steps):
        last = index == len(steps) - 1
        target = left if last else powers.at[index % 2]
        if mixed is not None:
            set_factors(*mixed)
        for f in range(fields):
            if multiplied is not None:
                multiply(f, multiplied[1], target)
            if mixed is not None:
                mix_lines(mixed[1], range(f * groups, (f + 1) * groups), current)
        if mixed is not None:
            written.add(mixed[1])
        current = target
    for half in range(HALVES if moves else 0):
        if half not in written:
            at = slice(half * width, (half + 1) * width)
            out[:, :, at] = state[:, :, at]


def advance(coef, height, held, count):
    fields = coef.shape[0]
    value = mix(coef, [held[f, 5 : 5 + count, :] for f in range(fields)])
    value = [held[f, 6 : 6 + count, :] + height / 3.0 * value[f] for f in range(fields)]
    value = mix(coef, value)
    value = [held[f, 7 : 7 + count, :] + height / 2.0 * value[f] for f in range(fields)]
    value = mix(coef, value)
    return [held[f, 8 : 8 + count, :] + height * value[f] for f in range(fields)]


def lift_kernel(coef, heights, weights0, weights1, lcols, state, out, held):
    fields, _, _ = out.shape
    held[...] = jnp.zeros_like(held)
    for f in range(fields):
        held[f, 8:11, :] = weights0[f, 0:3, :]
    value = advance(coef, heights[1:2, :], held, 6)
    for f in range(fields):
        held[f, 8:14, :] = value[f]
        held[f, 8:11, :] = held[f, 8:11, :] + weights1[f, 0:3, :]
    value = advance(coef, heights[2:3, :], held, 9)
    high, low = split(lcols[...])
    left = jnp.concatenate([high, high, low], axis=1)
    for f in range(fields):
        held[f, 8:17, :] = value[f]
        right_high, right_low = split(held[f, 8:24, :])
        right = jnp.concatenate([right_high, right_low, right_high], axis=0)
        out[f] = state[f] + jnp.dot(left, right, preferred_element_type=F32)


def closing_kernel(level, coef, heights, kappas, old_aux, lcols, state, member, *rest):
    tables = rest[:SLOTS]
    out, table, held, wide, sems = rest[SLOTS:]
    fields, basis, n_elem = state.shape
    means = gather([t[...] for t in tables], table, member[...])
    height = heights[level : level + 1, :]
    weights = lift_weights(coef, height, means, old_aux, kappas)
    for k in range(3):
        wide[k] = jnp.broadcast_to(lcols[:, k : k + 1], (basis, 128))
    copies = []
    for f in range(fields):
        for pair in range(n_elem // 256):
            lanes = [
                slice(pair * 256 + part * 128, pair * 256 + part * 128 + 128) for part in range(2)
            ]
            scale = [
                [jnp.broadcast_to(weights[f][k][:, at], (8, 128)) for k in range(3)]
                for at in lanes
            ]
            for group in range(basis // 8):
                lines = slice(group * 8, group * 8 + 8)
                vector = [wide[k, lines, :] for k in range(3)]
                for part in range(2):
                    value = state[f, lines, lanes[part]]
                    for k in range(3):
                        value = value + vector[k] * scale[part][k]
                    held[f, lines, lanes[part]] = value
        copies.append(pltpu.make_async_copy(held.at[f], out.at[f], sems.at[f]))
        copies[-1].start()
    for copy in copies:
        copy.wait()


def call(kernel, outs, args, scratch=(), scalars=0, flops=1000000, space=pltpu.VMEM, out_space=pltpu.VMEM, limit=40):
    specs = [
        pl.BlockSpec(memory_space=pltpu.SMEM if i < scalars else space)
        for i in range(len(args))
    ]
    single = not isinstance(outs, (list, tuple))
    shapes = [outs] if single else list(outs)
    moved = sum(4 * s.size for s in shapes) + sum(4 * a.size for a in args)
    result = pl.pallas_call(
        kernel,
        out_shape=shapes,
        in_specs=specs,
        out_specs=[pl.BlockSpec(memory_space=out_space)] * len(shapes),
        scratch_shapes=list(scratch),
        cost_estimate=pl.CostEstimate(flops=flops, bytes_accessed=moved, transcendentals=0),
        compiler_params=pltpu.CompilerParams(vmem_limit_bytes=min(limit * 1024 * 1024, 67043328)),
    )(*args)
    return result[0] if single else result


def shaped(*dims, dtype=F32):
    return jax.ShapeDtypeStruct(dims, dtype)


def swap(x, axis, odd):
    size = lax.axis_size(axis)
    pairs = []
    for i in range(size):
        mate = (i - 1 + 2 * (i % 2)) % size if odd else i + 1 - 2 * (i % 2)
        pairs.append((i, mate))
    return lax.ppermute(x, axis, pairs)


ROUTES = ((1, "gx", True), (0, "gx", False), (3, "gy", True), (2, "gy", False))


def exchange(pieces):
    received = [None] * 4
    for slot, axis, odd in ROUTES:
        received[slot] = swap(pieces[slot], axis, odd)
    return received


PARTS = ((0, 1), (1, 3), (3, 4), (4, 6), (6, 7))


def poly_steps(levels):
    blocks = [(level, half) for level in range(levels) for half in range(HALVES)]
    return list(zip([None] + blocks, blocks + [None]))


def slab(state, coef, basis_quad, test_deriv, trace_vec, lift_vec, tent_height, elem_tent):
    size_first = lax.axis_size("gx")
    size_second = lax.axis_size("gy")
    fields, basis, n_elem = state.shape
    levels, tent_dev = tent_height.shape
    shape = (size_first, size_second, tent_dev)
    me = (lax.axis_index("gx") * size_second + lax.axis_index("gy")).reshape(1)
    message = [shaped(ROWS // 2, 2 * tent_dev)] * SLOTS
    aux_shape = shaped(BACK, n_elem)
    vals = pltpu.VMEM((ROWS, n_elem), F32)
    table = pltpu.VMEM((BACK, SLOTS * tent_dev), F32)

    kept = [
        shaped(*basis_quad.shape),
        shaped(*test_deriv.shape[::-1]),
        shaped(*state.shape),
        shaped(*coef.shape),
        shaped(*elem_tent.shape, dtype=jnp.int32),
    ]
    rows3, lift, aux, *out = call(
        functools.partial(opening_kernel, shape),
        [shaped(8, basis), shaped(1, basis), aux_shape] + message + kept,
        (
            me,
            *(
                pltpu.with_memory_space_constraint(x, pltpu.HBM)
                for x in (
                    basis_quad,
                    test_deriv.T,
                    trace_vec,
                    lift_vec,
                    state,
                    coef,
                    tent_height,
                    elem_tent,
                )
            ),
        ),
        [
            vals,
            pltpu.VMEM(trace_vec.shape, F32),
            pltpu.VMEM(lift_vec.shape, F32),
            pltpu.VMEM(tent_height.shape, F32),
            pltpu.VMEM((3, basis, 128), F32),
            pltpu.VMEM((fields, 8, n_elem), F32),
            pltpu.SemaphoreType.DMA((8,)),
        ],
        1,
        space=pltpu.HBM,
    )
    basis_near, test_near, state, coef, elem_tent = out[SLOTS:]
    out = out[:SLOTS]
    stack, rstack, lcols, kappas = call(
        powers_kernel,
        [
            shaped(768, 256, dtype=BF16),
            shaped(32, 256, dtype=BF16),
            shaped(basis, 16),
            shaped(16, n_elem),
        ],
        (basis_near, test_near, rows3, lift),
        [
            pltpu.VMEM((16, basis), F32),
            pltpu.VMEM((8 + 2 * basis, basis), F32),
            pltpu.VMEM((basis, basis + 8), F32),
        ],
        flops=100000000,
    )
    proj = call(
        projections_kernel,
        shaped(fields, 16, n_elem),
        (rstack, state),
        [pltpu.VMEM((256, 256), BF16)],
        flops=300000000,
    )
    width = n_elem // HALVES
    weights = []
    heights = None
    steps = poly_steps(levels)
    values = state
    held = []

    def advance_state(values, held, part):
        chosen = PARTS[part]
        resumed = chosen[0] > 0
        mine = steps[chosen[0] : chosen[1]]
        half_powers = shaped(fields, 384, width)
        moves = any(mixed is not None for mixed, _ in mine)
        outs = [shaped(fields, basis, n_elem)] if moves else []
        if mine[-1][1] is not None:
            outs.append(half_powers)
        held = call(
            functools.partial(poly_kernel, mine, resumed),
            outs,
            (values, coef, heights, stack, *held),
            [
                pltpu.VMEM((2, 256, width), BF16),
                pltpu.VMEM((2, fields, 384, width), F32),
                pltpu.VMEM((fields * fields, 8, width), F32),
            ],
            flops=3000000000,
        )
        if moves:
            values, *held = held
        return values, held

    for level in range(levels):
        received = exchange(out[:4])
        means = call(owner_kernel, shaped(BACK, tent_dev), (kappas, out[4], *received))
        back = exchange([means] * 4)
        if level == 0:
            memberships = call(
                functools.partial(members_kernel, shape),
                [shaped(SLOTS * tent_dev, n_elem, dtype=BF16)] * levels,
                (me, elem_tent),
                (),
                1,
            )
            heights = call(
                lambda *refs: heights_kernel(refs[:5], refs[5 : 5 + levels], *refs[5 + levels :]),
                shaped(8, n_elem),
                (*received, out[4], *memberships),
                [table],
                flops=10000000,
            )
        if level < levels - 1:
            count = 6 - 3 * level
            drift = call(
                functools.partial(drift_kernel, level, count),
                shaped(fields, 8, n_elem),
                (coef, heights, proj),
            )
        if level < levels - 1:
            more = [shaped(fields, 8, n_elem)] if level < levels - 2 else []
            weight, aux, *out = call(
                functools.partial(element_kernel, level, count),
                [shaped(fields, 8, n_elem), aux_shape] + message + more,
                (
                    coef,
                    heights,
                    kappas,
                    aux,
                    drift,
                    memberships[level],
                    memberships[level + 1],
                    *back,
                    means,
                ),
                [vals, table],
            )
            weights.append(weight)
            if more:
                proj = out.pop()
    for part in range(len(PARTS)):
        values, held = advance_state(values, held, part)
    values = call(
        lift_kernel,
        shaped(fields, basis, n_elem),
        (coef, heights, weights[0], weights[1], lcols, values),
        [pltpu.VMEM((fields, 24, n_elem), F32)],
        flops=100000000,
    )
    return call(
        functools.partial(closing_kernel, levels - 1),
        shaped(fields, basis, n_elem),
        (coef, heights, kappas, aux, lcols, values, memberships[levels - 1], *back, means),
        [
            table,
            pltpu.VMEM(state.shape, F32),
            pltpu.VMEM((3, basis, 128), F32),
            pltpu.SemaphoreType.DMA((fields,)),
        ],
        out_space=pltpu.HBM,
    )


def solution(mesh):
    placed = (
        P(None, None, ("gx", "gy")),
        P(None, None, ("gx", "gy")),
        P(),
        P(),
        P(),
        P(),
        P(None, ("gx", "gy")),
        P(None, ("gx", "gy")),
    )
    return jax.shard_map(
        slab,
        mesh=mesh,
        in_specs=placed,
        out_specs=P(None, None, ("gx", "gy")),
        check_vma=False,
    )
```

```python
import functools

import jax
import jax.numpy as jnp
from jax import lax
from jax.experimental import pallas as pl
from jax.experimental.pallas import tpu as pltpu
from jax.sharding import PartitionSpec as P


F32 = jnp.float32
BF16 = jnp.bfloat16
HIGHEST = lax.Precision.HIGHEST
ROWS = 48
BACK = 16
SLOTS = 5
HALVES = 2


def split(x):
    high = x.astype(BF16)
    return high, (x - high.astype(F32)).astype(BF16)


def exact_dot(left, right):
    return jnp.dot(left, right, precision=HIGHEST, preferred_element_type=F32)


def partners(index, size):
    even = index + 1 - 2 * lax.rem(index, 2)
    odd = lax.rem(index - 1 + 2 * lax.rem(index, 2) + size, size)
    return even, odd


def tent_columns(tents, me, size_first, size_second, tent_dev):
    first = lax.div(me, size_second)
    second = lax.rem(me, size_second)
    first_even, first_odd = partners(first, size_first)
    second_even, second_odd = partners(second, size_second)
    owners = [
        first_even * size_second + second,
        first_odd * size_second + second,
        first * size_second + second_even,
        first * size_second + second_odd,
    ]
    column = tents - (me - 4) * tent_dev
    for slot, owner in enumerate(owners):
        inside = (tents >= owner * tent_dev) & (tents < (owner + 1) * tent_dev)
        column = jnp.where(inside, tents - (owner - slot) * tent_dev, column)
    return column


def members(tents, me, shape):
    size_first, size_second, tent_dev = shape
    column = tent_columns(tents, me, size_first, size_second, tent_dev)
    full = (SLOTS * tent_dev, column.shape[1])
    lines = lax.broadcasted_iota(jnp.int32, full, 0)
    return jnp.where(lines == column, 1.0, 0.0).astype(BF16)


def mix(coef, values):
    mixed = []
    for target in range(len(values)):
        total = coef[target, 0:1, :] * values[0]
        for source in range(1, len(values)):
            total = total + coef[target, source : source + 1, :] * values[source]
        mixed.append(total)
    return mixed


def tent_sums(coef, member, traces, aux, vals, messages, heights, kappa):
    fields = len(traces)
    once = mix(coef, traces)
    twice = mix(coef, once)
    vals[...] = jnp.zeros_like(vals)
    aux[...] = jnp.zeros_like(aux)
    for f in range(fields):
        vals[f : f + 1, :] = traces[f][0:1]
        vals[5 + f : 6 + f, :] = once[f][1:2]
        vals[10 + f : 11 + f, :] = twice[f][2:3] - kappa * once[f][0:1]
        vals[15 + 5 * f : 20 + 5 * f, :] = coef[f]
        aux[f : f + 1, :] = traces[f][0:1]
        aux[5 + f : 6 + f, :] = once[f][1:2]
        aux[10 + f : 11 + f, :] = twice[f][2:3]
    vals[40:41, :] = jnp.ones_like(vals[40:41, :])
    high, low = split(vals[...])
    both = jnp.concatenate([high, low], axis=0)
    sums = lax.dot_general(
        both, member, (((1,), (1,)), ((), ())), preferred_element_type=F32
    )
    sums = sums[:ROWS] + sums[ROWS:]
    rows, tent_dev = messages[0].shape[0], messages[0].shape[1] // 2
    for slot in range(SLOTS):
        columns = slice(slot * tent_dev, (slot + 1) * tent_dev)
        messages[slot][:, :tent_dev] = sums[:rows, columns]
        messages[slot][:, tent_dev:] = sums[rows:, columns]
        if heights is not None:
            messages[slot][41 - rows : 44 - rows, tent_dev:] = heights[...]


def opening_kernel(shape, me, basis_in, test_in, trace_in, lift_in, state_in, coef_in, *rest):
    heights_in, tents_in, rows3, lift_row, aux, *rest = rest
    messages = rest[:SLOTS]
    basis, test, state, coef, tents, *rest = rest[SLOTS:]
    vals, trace, lift, heights, wide, found, sems = rest
    sources = (test_in, trace_in, basis_in, lift_in, tents_in, state_in, coef_in, heights_in)
    targets = (test, trace, basis, lift, tents, state, coef, heights)
    copies = [
        pltpu.make_async_copy(source, target, sems.at[k])
        for k, (source, target) in enumerate(zip(sources, targets))
    ]
    for copy in copies:
        copy.start()
    count = trace.shape[0]
    copies[4].wait()
    member = members(tents[0:1, :], me[0], shape)
    for k in range(4):
        copies[k].wait()
    row = trace[...].reshape(1, count)
    rows3[...] = jnp.zeros_like(rows3)
    rows3[0:1, :] = row
    for k in (1, 2):
        tested = jnp.sum(test[...] * row, axis=1, keepdims=True)
        row = jnp.sum(basis[...] * tested, axis=0, keepdims=True)
        rows3[k : k + 1, :] = row
    lift_row[...] = lift[...].reshape(1, count)
    kappa = jnp.sum(rows3[1:2, :] * lift_row[...], axis=1, keepdims=True)
    columns = rows3[...].T
    for k in range(3):
        wide[k] = jnp.broadcast_to(columns[:, k : k + 1], (count, 128))
    copies[5].wait()
    fields = state.shape[0]
    for pair in range(state.shape[2] // 256):
        lanes = [slice(pair * 256 + part * 128, pair * 256 + part * 128 + 128) for part in range(2)]
        totals = {}
        for group in range(count // 8):
            lines = slice(group * 8, group * 8 + 8)
            vector = [wide[k, lines, :] for k in range(3)]
            for f in range(fields):
                for part in range(2):
                    block = state[f, lines, lanes[part]]
                    for k in range(3):
                        term = block * vector[k]
                        held = totals.get((f, part, k))
                        totals[f, part, k] = term if held is None else held + term
        for (f, part, k), total in totals.items():
            found[f, k : k + 1, lanes[part]] = jnp.sum(total, axis=0, keepdims=True)
    copies[6].wait()
    copies[7].wait()
    traces = [found[f, 0:3, :] for f in range(fields)]
    tent_sums(coef, member, traces, aux, vals, messages, heights, kappa)


def powers_kernel(basis, test, rows3, lift, stack, rstack, lcols, kappas, rows, left, right):
    count = basis.shape[1]
    first, second = slice(8, 8 + count), slice(8 + count, 8 + 2 * count)
    extra = right.shape[1]
    s1 = lax.dot_general(
        test[...],
        basis[...],
        (((0,), (0,)), ((), ())),
        precision=HIGHEST,
        preferred_element_type=F32,
    )
    stack[...] = jnp.zeros_like(stack)
    rstack[...] = jnp.zeros_like(rstack)
    rows[...] = jnp.zeros_like(rows)
    left[...] = jnp.zeros_like(left)
    right[...] = jnp.zeros_like(right)
    lcols[...] = jnp.zeros_like(lcols)
    rows[8:9, :] = lift[...]
    lcols[:, 0:8] = rows[8:16, :].T
    rows[0:3, :] = rows3[0:3, :]
    left[0:8, :] = rows[0:8, :]
    left[first, :] = s1
    right[:, 0:count] = s1
    right[:, count:extra] = lcols[:, 0:8]
    product = exact_dot(left[0 : 8 + count, :], right[...])
    s2 = product[first, 0:count]
    rows[3:4, :] = product[2:3, 0:count]
    lcols[:, 1:2] = product[first, count : count + 1]
    left[0:8, :] = rows[0:8, :]
    left[second, :] = s2
    right[:, 0:count] = s2
    right[:, count:extra] = lcols[:, 0:8]
    product = exact_dot(left[0 : 8 + 2 * count, :], right[...])
    s3 = product[first, 0:count]
    s4 = product[second, 0:count]
    rows[4:6, :] = product[2:4, 0:count]
    lcols[:, 2:4] = product[second, count : count + 2]
    left[0:4, :] = rows[2:6, :]
    left[first, :] = s4
    right[:, 0:count] = s4
    right[:, count:extra] = lcols[:, 0:8]
    product = exact_dot(left[0 : 8 + count, :], right[...])
    rows[6:9, :] = product[0:3, 0:count]
    lcols[:, 4:8] = product[first, count : count + 4]
    lcols[:, 8:9] = jnp.sum(product[first, 0:count] * lift[...], axis=1, keepdims=True)
    kappas[...] = jnp.broadcast_to(
        jnp.sum(rows[...] * lift[...], axis=1, keepdims=True), kappas.shape
    )
    half = rstack.shape[1] // 2
    row_high, row_low = split(rows[...])
    for side in range(2):
        columns = slice(side * half, side * half + count)
        for power, matrix in enumerate((s1, s2 / 2.0, s3 / 6.0)):
            high, low = split(matrix)
            stack[power * half : power * half + count, columns] = high
            stack[(3 + power) * half : (3 + power) * half + count, columns] = low
        rstack[0:16, columns] = row_high
        rstack[16:32, columns] = row_low


def projections_kernel(rstack, state, out, packed):
    fields, count, n_elem = state.shape
    width = packed.shape[1]
    half = packed.shape[0] // 2
    packed[...] = jnp.zeros_like(packed)
    for f in range(fields):
        for block in range(n_elem // width):
            at = slice(block * width, (block + 1) * width)
            high, low = split(state[f, :, at])
            packed[0:count, :] = high
            packed[half : half + count, :] = low
            product = jnp.dot(rstack[...], packed[...], preferred_element_type=F32)
            out[f, :, at] = product[:16] + product[16:]


def owner_kernel(kappas, own, *rest):
    *received, out = rest
    total = own[...]
    for ref in received:
        total = total + ref[...]
    total = jnp.concatenate([total[:, : out.shape[1]], total[:, out.shape[1] :]], axis=0)
    mean = total / jnp.maximum(total[40:41], 1.0)
    first = mean[0:5]
    out[...] = jnp.zeros_like(out)
    out[0:10, :] = mean[0:10]
    kappa = kappas[1:2, 0 : out.shape[1]]
    for g in range(5):
        moved = jnp.sum(mean[15 + 5 * g : 20 + 5 * g] * first, axis=0, keepdims=True)
        out[10 + g : 11 + g, :] = mean[10 + g : 11 + g] + kappa * moved


def gather(tables, table, member):
    tent_dev = table.shape[1] // SLOTS
    for slot in range(SLOTS):
        table[:, slot * tent_dev : (slot + 1) * tent_dev] = tables[slot]
    high, low = split(table[...])
    found = jnp.dot(
        jnp.concatenate([high, low], axis=0), member, preferred_element_type=F32
    )
    count = table.shape[0]
    return found[:count] + found[count:]


def members_kernel(shape, me, tents, *outs):
    for level, out in enumerate(outs):
        out[...] = members(tents[level : level + 1, :], me[0], shape)


def heights_kernel(messages, memberships, out, table):
    out[...] = jnp.zeros_like(out)
    half = messages[0].shape[1] // 2
    for level, member in enumerate(memberships):
        found = gather([m[8:24, half:] for m in messages], table, member[...])
        out[level : level + 1, :] = found[9 + level : 10 + level]


def drift_kernel(level, count, coef, heights, proj, out):
    fields = coef.shape[0]
    height = heights[level : level + 1, :]
    state = mix(coef, [proj[f, 3 : 3 + count, :] for f in range(fields)])
    state = [proj[f, 2 : 2 + count, :] + height / 3.0 * state[f] for f in range(fields)]
    state = mix(coef, state)
    state = [proj[f, 1 : 1 + count, :] + height / 2.0 * state[f] for f in range(fields)]
    state = mix(coef, state)
    for f in range(fields):
        out[f, 0:count, :] = proj[f, 0:count, :] + height * state[f]


def lift_weights(coef, height, means, aux, kappas):
    kappa0 = kappas[0:1, :]
    kappa1 = kappas[1:2, :]
    fields = coef.shape[0]
    first = [means[f : f + 1] - aux[f : f + 1, :] for f in range(fields)]
    second = [
        means[5 + f : 6 + f] - aux[5 + f : 6 + f, :] - kappa0 * first[f] for f in range(fields)
    ]
    moved = mix(coef, [jnp.concatenate([first[f], second[f]], axis=0) for f in range(fields)])
    moved_first = [m[0:1] for m in moved]
    moved_second = [m[1:2] for m in moved]
    moved_twice = mix(coef, moved_first)
    half = height * height / 2.0
    sixth = height * height * height / 6.0
    weights = []
    for f in range(fields):
        third = (
            means[10 + f : 11 + f]
            - aux[10 + f : 11 + f, :]
            - kappa1 * moved_first[f]
            - kappa0 * second[f]
        )
        weights.append(
            (
                height * first[f] + half * second[f] + sixth * third,
                half * moved_first[f] + sixth * moved_second[f],
                sixth * moved_twice[f],
            )
        )
    return weights


def element_kernel(level, count, coef, heights, kappas, old_aux, drift, member, following, *rest):
    tables = rest[:SLOTS]
    weights_out, aux, *messages = rest[SLOTS : 2 * SLOTS + 2]
    proj_out = rest[2 * SLOTS + 2] if count > 3 else None
    vals, table = rest[-2:]
    fields = coef.shape[0]
    means = gather([t[...] for t in tables], table, member[...])
    height = heights[level : level + 1, :]
    weights = lift_weights(coef, height, means, old_aux, kappas)
    weights_out[...] = jnp.zeros_like(weights_out)
    fresh = []
    for f in range(fields):
        for k in range(3):
            weights_out[f, k : k + 1, :] = weights[f][k]
        value = drift[f, 0:count, :]
        for k in range(3):
            value = value + kappas[k : k + count, :] * weights[f][k]
        fresh.append(value)
        if proj_out is not None:
            proj_out[f, 0:count, :] = value
    tent_sums(
        coef,
        following[...],
        [v[0:3] for v in fresh],
        aux,
        vals,
        messages,
        None,
        kappas[1:2, :],
    )


def poly_kernel(steps, resumed, state, coef, heights, stack, *rest):
    rest = list(rest)
    current = rest.pop(0) if resumed else None
    moves = any(mixed is not None for mixed, _ in steps)
    out = rest.pop(0) if moves else None
    left = rest.pop(0) if steps[-1][1] is not None else None
    packed, powers, factors = rest
    fields, basis, n_elem = state.shape
    width = n_elem // HALVES
    half_rows = packed.shape[1] // 2
    written = set()
    packed[...] = jnp.zeros_like(packed)

    def multiply(f, half, target):
        source = out if half in written else state
        high, low = split(source[f, :, half * width : (half + 1) * width])
        slot = f % 2
        packed[slot, 0:basis, :] = high
        packed[slot, half_rows : half_rows + basis, :] = low
        product = jnp.dot(stack[...], packed[slot], preferred_element_type=F32)
        target[f] = product[: 3 * half_rows] + product[3 * half_rows :]

    def set_factors(level, half):
        at = slice(half * width, (half + 1) * width)
        height = heights[level : level + 1, at]
        for g in range(fields):
            for f in range(fields):
                factors[g * fields + f] = jnp.broadcast_to(
                    height * coef[g, f : f + 1, at], (8, width)
                )

    def mix_lines(half, groups, values):
        base = out if half in written else state
        for tile in range(width // 128):
            near = slice(tile * 128, (tile + 1) * 128)
            at = slice(half * width + tile * 128, half * width + (tile + 1) * 128)
            factor = [factors[k, :, near] for k in range(fields * fields)]

            def combine(start, values):
                mixed = []
                for g in range(fields):
                    total = start[g]
                    for f in range(fields):
                        total = total + factor[g * fields + f] * values[f]
                    mixed.append(total)
                return mixed

            for group in groups:
                lines = slice(group * 8, group * 8 + 8)

                def power(k):
                    rows = slice(k * half_rows + group * 8, k * half_rows + group * 8 + 8)
                    return [values[f, rows, near] for f in range(fields)]

                value = combine(power(1), power(2))
                value = combine(power(0), value)
                value = combine([base[f, lines, at] for f in range(fields)], value)
                for f in range(fields):
                    out[f, lines, at] = value[f]

    groups = basis // 8 // fields
    for index, (mixed, multiplied) in enumerate(steps):
        last = index == len(steps) - 1
        target = left if last else powers.at[index % 2]
        if mixed is not None:
            set_factors(*mixed)
        for f in range(fields):
            if multiplied is not None:
                multiply(f, multiplied[1], target)
            if mixed is not None:
                mix_lines(mixed[1], range(f * groups, (f + 1) * groups), current)
        if mixed is not None:
            written.add(mixed[1])
        current = target
    for half in range(HALVES if moves else 0):
        if half not in written:
            at = slice(half * width, (half + 1) * width)
            out[:, :, at] = state[:, :, at]


def advance(coef, height, held, count):
    fields = coef.shape[0]
    value = mix(coef, [held[f, 5 : 5 + count, :] for f in range(fields)])
    value = [held[f, 6 : 6 + count, :] + height / 3.0 * value[f] for f in range(fields)]
    value = mix(coef, value)
    value = [held[f, 7 : 7 + count, :] + height / 2.0 * value[f] for f in range(fields)]
    value = mix(coef, value)
    return [held[f, 8 : 8 + count, :] + height * value[f] for f in range(fields)]


def lift_kernel(coef, heights, weights0, weights1, lcols, state, out, held):
    fields, _, _ = out.shape
    held[...] = jnp.zeros_like(held)
    for f in range(fields):
        held[f, 8:11, :] = weights0[f, 0:3, :]
    value = advance(coef, heights[1:2, :], held, 6)
    for f in range(fields):
        held[f, 8:14, :] = value[f]
        held[f, 8:11, :] = held[f, 8:11, :] + weights1[f, 0:3, :]
    value = advance(coef, heights[2:3, :], held, 9)
    high, low = split(lcols[...])
    left = jnp.concatenate([high, high, low], axis=1)
    for f in range(fields):
        held[f, 8:17, :] = value[f]
        right_high, right_low = split(held[f, 8:24, :])
        right = jnp.concatenate([right_high, right_low, right_high], axis=0)
        out[f] = state[f] + jnp.dot(left, right, preferred_element_type=F32)


def closing_kernel(level, coef, heights, kappas, old_aux, lcols, state, member, *rest):
    tables = rest[:SLOTS]
    out, table, held, wide, scales, sems = rest[SLOTS:]
    fields, basis, n_elem = state.shape
    means = gather([t[...] for t in tables], table, member[...])
    height = heights[level : level + 1, :]
    weights = lift_weights(coef, height, means, old_aux, kappas)
    for k in range(3):
        wide[k] = jnp.broadcast_to(lcols[:, k : k + 1], (basis, 128))
    for f in range(fields):
        for k in range(3):
            scales[f, k : k + 1, :] = weights[f][k]

    def field(f, carry):
        for pair in range(n_elem // 256):
            lanes = [
                slice(pair * 256 + part * 128, pair * 256 + part * 128 + 128) for part in range(2)
            ]
            scale = [
                [jnp.broadcast_to(scales[f, k : k + 1, at], (8, 128)) for k in range(3)]
                for at in lanes
            ]
            for group in range(basis // 8):
                lines = slice(group * 8, group * 8 + 8)
                vector = [wide[k, lines, :] for k in range(3)]
                for part in range(2):
                    value = state[f, lines, lanes[part]]
                    for k in range(3):
                        value = value + vector[k] * scale[part][k]
                    held[f, lines, lanes[part]] = value
        pltpu.make_async_copy(held.at[f], out.at[f], sems.at[f]).start()
        return carry

    lax.fori_loop(0, fields, field, 0)
    for f in range(fields):
        pltpu.make_async_copy(held.at[f], out.at[f], sems.at[f]).wait()


def call(kernel, outs, args, scratch=(), scalars=0, flops=1000000, space=pltpu.VMEM, out_space=pltpu.VMEM, limit=40):
    specs = [
        pl.BlockSpec(memory_space=pltpu.SMEM if i < scalars else space)
        for i in range(len(args))
    ]
    single = not isinstance(outs, (list, tuple))
    shapes = [outs] if single else list(outs)
    moved = sum(4 * s.size for s in shapes) + sum(4 * a.size for a in args)
    result = pl.pallas_call(
        kernel,
        out_shape=shapes,
        in_specs=specs,
        out_specs=[pl.BlockSpec(memory_space=out_space)] * len(shapes),
        scratch_shapes=list(scratch),
        cost_estimate=pl.CostEstimate(flops=flops, bytes_accessed=moved, transcendentals=0),
        compiler_params=pltpu.CompilerParams(vmem_limit_bytes=min(limit * 1024 * 1024, 67043328)),
    )(*args)
    return result[0] if single else result


def shaped(*dims, dtype=F32):
    return jax.ShapeDtypeStruct(dims, dtype)


def swap(x, axis, odd):
    size = lax.axis_size(axis)
    pairs = []
    for i in range(size):
        mate = (i - 1 + 2 * (i % 2)) % size if odd else i + 1 - 2 * (i % 2)
        pairs.append((i, mate))
    return lax.ppermute(x, axis, pairs)


ROUTES = ((1, "gx", True), (0, "gx", False), (3, "gy", True), (2, "gy", False))


def exchange(pieces):
    received = [None] * 4
    for slot, axis, odd in ROUTES:
        received[slot] = swap(pieces[slot], axis, odd)
    return received


PARTS = ((0, 1), (1, 3), (3, 4), (4, 6), (6, 7))


def poly_steps(levels):
    blocks = [(level, half) for level in range(levels) for half in range(HALVES)]
    return list(zip([None] + blocks, blocks + [None]))


def slab(state, coef, basis_quad, test_deriv, trace_vec, lift_vec, tent_height, elem_tent):
    size_first = lax.axis_size("gx")
    size_second = lax.axis_size("gy")
    fields, basis, n_elem = state.shape
    levels, tent_dev = tent_height.shape
    shape = (size_first, size_second, tent_dev)
    me = (lax.axis_index("gx") * size_second + lax.axis_index("gy")).reshape(1)
    message = [shaped(ROWS // 2, 2 * tent_dev)] * SLOTS
    aux_shape = shaped(BACK, n_elem)
    vals = pltpu.VMEM((ROWS, n_elem), F32)
    table = pltpu.VMEM((BACK, SLOTS * tent_dev), F32)

    kept = [
        shaped(*basis_quad.shape),
        shaped(*test_deriv.shape[::-1]),
        shaped(*state.shape),
        shaped(*coef.shape),
        shaped(*elem_tent.shape, dtype=jnp.int32),
    ]
    rows3, lift, aux, *out = call(
        functools.partial(opening_kernel, shape),
        [shaped(8, basis), shaped(1, basis), aux_shape] + message + kept,
        (
            me,
            *(
                pltpu.with_memory_space_constraint(x, pltpu.HBM)
                for x in (
                    basis_quad,
                    test_deriv.T,
                    trace_vec,
                    lift_vec,
                    state,
                    coef,
                    tent_height,
                    elem_tent,
                )
            ),
        ),
        [
            vals,
            pltpu.VMEM(trace_vec.shape, F32),
            pltpu.VMEM(lift_vec.shape, F32),
            pltpu.VMEM(tent_height.shape, F32),
            pltpu.VMEM((3, basis, 128), F32),
            pltpu.VMEM((fields, 8, n_elem), F32),
            pltpu.SemaphoreType.DMA((8,)),
        ],
        1,
        space=pltpu.HBM,
    )
    basis_near, test_near, state, coef, elem_tent = out[SLOTS:]
    out = out[:SLOTS]
    stack, rstack, lcols, kappas = call(
        powers_kernel,
        [
            shaped(768, 256, dtype=BF16),
            shaped(32, 256, dtype=BF16),
            shaped(basis, 16),
            shaped(16, n_elem),
        ],
        (basis_near, test_near, rows3, lift),
        [
            pltpu.VMEM((16, basis), F32),
            pltpu.VMEM((8 + 2 * basis, basis), F32),
            pltpu.VMEM((basis, basis + 8), F32),
        ],
        flops=100000000,
    )
    proj = call(
        projections_kernel,
        shaped(fields, 16, n_elem),
        (rstack, state),
        [pltpu.VMEM((256, 256), BF16)],
        flops=300000000,
    )
    width = n_elem // HALVES
    weights = []
    heights = None
    steps = poly_steps(levels)
    values = state
    held = []

    def advance_state(values, held, part):
        chosen = PARTS[part]
        resumed = chosen[0] > 0
        mine = steps[chosen[0] : chosen[1]]
        half_powers = shaped(fields, 384, width)
        moves = any(mixed is not None for mixed, _ in mine)
        outs = [shaped(fields, basis, n_elem)] if moves else []
        if mine[-1][1] is not None:
            outs.append(half_powers)
        held = call(
            functools.partial(poly_kernel, mine, resumed),
            outs,
            (values, coef, heights, stack, *held),
            [
                pltpu.VMEM((2, 256, width), BF16),
                pltpu.VMEM((2, fields, 384, width), F32),
                pltpu.VMEM((fields * fields, 8, width), F32),
            ],
            flops=3000000000,
        )
        if moves:
            values, *held = held
        return values, held

    for level in range(levels):
        received = exchange(out[:4])
        means = call(owner_kernel, shaped(BACK, tent_dev), (kappas, out[4], *received))
        back = exchange([means] * 4)
        if level == 0:
            memberships = call(
                functools.partial(members_kernel, shape),
                [shaped(SLOTS * tent_dev, n_elem, dtype=BF16)] * levels,
                (me, elem_tent),
                (),
                1,
            )
            heights = call(
                lambda *refs: heights_kernel(refs[:5], refs[5 : 5 + levels], *refs[5 + levels :]),
                shaped(8, n_elem),
                (*received, out[4], *memberships),
                [table],
                flops=10000000,
            )
        if level < levels - 1:
            count = 6 - 3 * level
            drift = call(
                functools.partial(drift_kernel, level, count),
                shaped(fields, 8, n_elem),
                (coef, heights, proj),
            )
        if level < levels - 1:
            more = [shaped(fields, 8, n_elem)] if level < levels - 2 else []
            weight, aux, *out = call(
                functools.partial(element_kernel, level, count),
                [shaped(fields, 8, n_elem), aux_shape] + message + more,
                (
                    coef,
                    heights,
                    kappas,
                    aux,
                    drift,
                    memberships[level],
                    memberships[level + 1],
                    *back,
                    means,
                ),
                [vals, table],
            )
            weights.append(weight)
            if more:
                proj = out.pop()
    for part in range(len(PARTS)):
        values, held = advance_state(values, held, part)
    values = call(
        lift_kernel,
        shaped(fields, basis, n_elem),
        (coef, heights, weights[0], weights[1], lcols, values),
        [pltpu.VMEM((fields, 24, n_elem), F32)],
        flops=100000000,
    )
    return call(
        functools.partial(closing_kernel, levels - 1),
        shaped(fields, basis, n_elem),
        (coef, heights, kappas, aux, lcols, values, memberships[levels - 1], *back, means),
        [
            table,
            pltpu.VMEM(state.shape, F32),
            pltpu.VMEM((3, basis, 128), F32),
            pltpu.VMEM((fields, 8, n_elem), F32),
            pltpu.SemaphoreType.DMA((fields,)),
        ],
        out_space=pltpu.HBM,
    )


def solution(mesh):
    placed = (
        P(None, None, ("gx", "gy")),
        P(None, None, ("gx", "gy")),
        P(),
        P(),
        P(),
        P(),
        P(None, ("gx", "gy")),
        P(None, ("gx", "gy")),
    )
    return jax.shard_map(
        slab,
        mesh=mesh,
        in_specs=placed,
        out_specs=P(None, None, ("gx", "gy")),
        check_vma=False,
    )
```

```python
import functools

import jax
import jax.numpy as jnp
from jax import lax
from jax.experimental import pallas as pl
from jax.experimental.pallas import tpu as pltpu
from jax.sharding import PartitionSpec as P


F32 = jnp.float32
BF16 = jnp.bfloat16
HIGHEST = lax.Precision.HIGHEST
ROWS = 48
BACK = 16
SLOTS = 5
HALVES = 2


def split(x):
    high = x.astype(BF16)
    return high, (x - high.astype(F32)).astype(BF16)


def exact_dot(left, right):
    return jnp.dot(left, right, precision=HIGHEST, preferred_element_type=F32)


def partners(index, size):
    even = index + 1 - 2 * lax.rem(index, 2)
    odd = lax.rem(index - 1 + 2 * lax.rem(index, 2) + size, size)
    return even, odd


def tent_columns(tents, me, size_first, size_second, tent_dev):
    first = lax.div(me, size_second)
    second = lax.rem(me, size_second)
    first_even, first_odd = partners(first, size_first)
    second_even, second_odd = partners(second, size_second)
    owners = [
        first_even * size_second + second,
        first_odd * size_second + second,
        first * size_second + second_even,
        first * size_second + second_odd,
    ]
    column = tents - (me - 4) * tent_dev
    for slot, owner in enumerate(owners):
        inside = (tents >= owner * tent_dev) & (tents < (owner + 1) * tent_dev)
        column = jnp.where(inside, tents - (owner - slot) * tent_dev, column)
    return column


def members(tents, me, shape):
    size_first, size_second, tent_dev = shape
    column = tent_columns(tents, me, size_first, size_second, tent_dev)
    full = (SLOTS * tent_dev, column.shape[1])
    lines = lax.broadcasted_iota(jnp.int32, full, 0)
    return jnp.where(lines == column, 1.0, 0.0).astype(BF16)


def mix(coef, values):
    mixed = []
    for target in range(len(values)):
        total = coef[target, 0:1, :] * values[0]
        for source in range(1, len(values)):
            total = total + coef[target, source : source + 1, :] * values[source]
        mixed.append(total)
    return mixed


def tent_sums(coef, member, traces, aux, vals, messages, heights, kappa):
    fields = len(traces)
    once = mix(coef, traces)
    twice = mix(coef, once)
    vals[...] = jnp.zeros_like(vals)
    aux[...] = jnp.zeros_like(aux)
    for f in range(fields):
        vals[f : f + 1, :] = traces[f][0:1]
        vals[5 + f : 6 + f, :] = once[f][1:2]
        vals[10 + f : 11 + f, :] = twice[f][2:3] - kappa * once[f][0:1]
        vals[15 + 5 * f : 20 + 5 * f, :] = coef[f]
        aux[f : f + 1, :] = traces[f][0:1]
        aux[5 + f : 6 + f, :] = once[f][1:2]
        aux[10 + f : 11 + f, :] = twice[f][2:3]
    vals[40:41, :] = jnp.ones_like(vals[40:41, :])
    high, low = split(vals[...])
    both = jnp.concatenate([high, low], axis=0)
    sums = lax.dot_general(
        both, member, (((1,), (1,)), ((), ())), preferred_element_type=F32
    )
    sums = sums[:ROWS] + sums[ROWS:]
    rows, tent_dev = messages[0].shape[0], messages[0].shape[1] // 2
    for slot in range(SLOTS):
        columns = slice(slot * tent_dev, (slot + 1) * tent_dev)
        messages[slot][:, :tent_dev] = sums[:rows, columns]
        messages[slot][:, tent_dev:] = sums[rows:, columns]
        if heights is not None:
            messages[slot][41 - rows : 44 - rows, tent_dev:] = heights[...]


def opening_kernel(shape, me, basis_in, test_in, trace_in, lift_in, state_in, coef_in, *rest):
    heights_in, tents_in, rows3, lift_row, aux, *rest = rest
    messages = rest[:SLOTS]
    basis, test, state, coef, tents, *rest = rest[SLOTS:]
    vals, trace, lift, heights, wide, found, sems = rest
    sources = (test_in, trace_in, basis_in, lift_in, tents_in, state_in, coef_in, heights_in)
    targets = (test, trace, basis, lift, tents, state, coef, heights)
    copies = [
        pltpu.make_async_copy(source, target, sems.at[k])
        for k, (source, target) in enumerate(zip(sources, targets))
    ]
    for copy in copies:
        copy.start()
    count = trace.shape[0]
    copies[4].wait()
    member = members(tents[0:1, :], me[0], shape)
    for k in range(4):
        copies[k].wait()
    row = trace[...].reshape(1, count)
    rows3[...] = jnp.zeros_like(rows3)
    rows3[0:1, :] = row
    for k in (1, 2):
        tested = jnp.sum(test[...] * row, axis=1, keepdims=True)
        row = jnp.sum(basis[...] * tested, axis=0, keepdims=True)
        rows3[k : k + 1, :] = row
    lift_row[...] = lift[...].reshape(1, count)
    kappa = jnp.sum(rows3[1:2, :] * lift_row[...], axis=1, keepdims=True)
    columns = rows3[...].T
    for k in range(3):
        wide[k] = jnp.broadcast_to(columns[:, k : k + 1], (count, 128))
    copies[5].wait()
    fields = state.shape[0]
    for pair in range(state.shape[2] // 256):
        lanes = [slice(pair * 256 + part * 128, pair * 256 + part * 128 + 128) for part in range(2)]
        totals = {}
        for group in range(count // 8):
            lines = slice(group * 8, group * 8 + 8)
            vector = [wide[k, lines, :] for k in range(3)]
            for f in range(fields):
                for part in range(2):
                    block = state[f, lines, lanes[part]]
                    for k in range(3):
                        term = block * vector[k]
                        held = totals.get((f, part, k))
                        totals[f, part, k] = term if held is None else held + term
        for (f, part, k), total in totals.items():
            found[f, k : k + 1, lanes[part]] = jnp.sum(total, axis=0, keepdims=True)
    copies[6].wait()
    copies[7].wait()
    traces = [found[f, 0:3, :] for f in range(fields)]
    tent_sums(coef, member, traces, aux, vals, messages, heights, kappa)


def powers_kernel(basis, test, rows3, lift, stack, rstack, lcols, kappas, rows, left, right):
    count = basis.shape[1]
    first, second = slice(8, 8 + count), slice(8 + count, 8 + 2 * count)
    extra = right.shape[1]
    s1 = lax.dot_general(
        test[...],
        basis[...],
        (((0,), (0,)), ((), ())),
        precision=HIGHEST,
        preferred_element_type=F32,
    )
    stack[...] = jnp.zeros_like(stack)
    rstack[...] = jnp.zeros_like(rstack)
    rows[...] = jnp.zeros_like(rows)
    left[...] = jnp.zeros_like(left)
    right[...] = jnp.zeros_like(right)
    lcols[...] = jnp.zeros_like(lcols)
    rows[8:9, :] = lift[...]
    lcols[:, 0:8] = rows[8:16, :].T
    rows[0:3, :] = rows3[0:3, :]
    left[0:8, :] = rows[0:8, :]
    left[first, :] = s1
    right[:, 0:count] = s1
    right[:, count:extra] = lcols[:, 0:8]
    product = exact_dot(left[0 : 8 + count, :], right[...])
    s2 = product[first, 0:count]
    rows[3:4, :] = product[2:3, 0:count]
    lcols[:, 1:2] = product[first, count : count + 1]
    left[0:8, :] = rows[0:8, :]
    left[second, :] = s2
    right[:, 0:count] = s2
    right[:, count:extra] = lcols[:, 0:8]
    product = exact_dot(left[0 : 8 + 2 * count, :], right[...])
    s3 = product[first, 0:count]
    s4 = product[second, 0:count]
    rows[4:6, :] = product[2:4, 0:count]
    lcols[:, 2:4] = product[second, count : count + 2]
    left[0:4, :] = rows[2:6, :]
    left[first, :] = s4
    right[:, 0:count] = s4
    right[:, count:extra] = lcols[:, 0:8]
    product = exact_dot(left[0 : 8 + count, :], right[...])
    rows[6:9, :] = product[0:3, 0:count]
    lcols[:, 4:8] = product[first, count : count + 4]
    lcols[:, 8:9] = jnp.sum(product[first, 0:count] * lift[...], axis=1, keepdims=True)
    kappas[...] = jnp.broadcast_to(
        jnp.sum(rows[...] * lift[...], axis=1, keepdims=True), kappas.shape
    )
    half = rstack.shape[1] // 2
    row_high, row_low = split(rows[...])
    for side in range(2):
        columns = slice(side * half, side * half + count)
        for power, matrix in enumerate((s1, s2 / 2.0, s3 / 6.0)):
            high, low = split(matrix)
            stack[power * half : power * half + count, columns] = high
            stack[(3 + power) * half : (3 + power) * half + count, columns] = low
        rstack[0:16, columns] = row_high
        rstack[16:32, columns] = row_low


def projections_kernel(rstack, state, out, packed):
    fields, count, n_elem = state.shape
    width = packed.shape[1]
    half = packed.shape[0] // 2
    packed[...] = jnp.zeros_like(packed)
    for f in range(fields):
        for block in range(n_elem // width):
            at = slice(block * width, (block + 1) * width)
            high, low = split(state[f, :, at])
            packed[0:count, :] = high
            packed[half : half + count, :] = low
            product = jnp.dot(rstack[...], packed[...], preferred_element_type=F32)
            out[f, :, at] = product[:16] + product[16:]


def owner_kernel(kappas, own, *rest):
    *received, out = rest
    total = own[...]
    for ref in received:
        total = total + ref[...]
    total = jnp.concatenate([total[:, : out.shape[1]], total[:, out.shape[1] :]], axis=0)
    mean = total / jnp.maximum(total[40:41], 1.0)
    first = mean[0:5]
    out[...] = jnp.zeros_like(out)
    out[0:10, :] = mean[0:10]
    kappa = kappas[1:2, 0 : out.shape[1]]
    for g in range(5):
        moved = jnp.sum(mean[15 + 5 * g : 20 + 5 * g] * first, axis=0, keepdims=True)
        out[10 + g : 11 + g, :] = mean[10 + g : 11 + g] + kappa * moved


def gather(tables, table, member):
    tent_dev = table.shape[1] // SLOTS
    for slot in range(SLOTS):
        table[:, slot * tent_dev : (slot + 1) * tent_dev] = tables[slot]
    high, low = split(table[...])
    found = jnp.dot(
        jnp.concatenate([high, low], axis=0), member, preferred_element_type=F32
    )
    count = table.shape[0]
    return found[:count] + found[count:]


def members_kernel(shape, me, tents, *outs):
    for level, out in enumerate(outs):
        out[...] = members(tents[level : level + 1, :], me[0], shape)


def heights_kernel(messages, memberships, out, table):
    out[...] = jnp.zeros_like(out)
    half = messages[0].shape[1] // 2
    for level, member in enumerate(memberships):
        found = gather([m[8:24, half:] for m in messages], table, member[...])
        out[level : level + 1, :] = found[9 + level : 10 + level]


def drift_kernel(level, count, coef, heights, proj, out):
    fields = coef.shape[0]
    height = heights[level : level + 1, :]
    state = mix(coef, [proj[f, 3 : 3 + count, :] for f in range(fields)])
    state = [proj[f, 2 : 2 + count, :] + height / 3.0 * state[f] for f in range(fields)]
    state = mix(coef, state)
    state = [proj[f, 1 : 1 + count, :] + height / 2.0 * state[f] for f in range(fields)]
    state = mix(coef, state)
    for f in range(fields):
        out[f, 0:count, :] = proj[f, 0:count, :] + height * state[f]


def lift_weights(coef, height, means, aux, kappas):
    kappa0 = kappas[0:1, :]
    kappa1 = kappas[1:2, :]
    fields = coef.shape[0]
    first = [means[f : f + 1] - aux[f : f + 1, :] for f in range(fields)]
    second = [
        means[5 + f : 6 + f] - aux[5 + f : 6 + f, :] - kappa0 * first[f] for f in range(fields)
    ]
    moved = mix(coef, [jnp.concatenate([first[f], second[f]], axis=0) for f in range(fields)])
    moved_first = [m[0:1] for m in moved]
    moved_second = [m[1:2] for m in moved]
    moved_twice = mix(coef, moved_first)
    half = height * height / 2.0
    sixth = height * height * height / 6.0
    weights = []
    for f in range(fields):
        third = (
            means[10 + f : 11 + f]
            - aux[10 + f : 11 + f, :]
            - kappa1 * moved_first[f]
            - kappa0 * second[f]
        )
        weights.append(
            (
                height * first[f] + half * second[f] + sixth * third,
                half * moved_first[f] + sixth * moved_second[f],
                sixth * moved_twice[f],
            )
        )
    return weights


def element_kernel(level, count, coef, heights, kappas, old_aux, drift, member, following, *rest):
    tables = rest[:SLOTS]
    weights_out, aux, *messages = rest[SLOTS : 2 * SLOTS + 2]
    proj_out = rest[2 * SLOTS + 2] if count > 3 else None
    vals, table = rest[-2:]
    fields = coef.shape[0]
    means = gather([t[...] for t in tables], table, member[...])
    height = heights[level : level + 1, :]
    weights = lift_weights(coef, height, means, old_aux, kappas)
    weights_out[...] = jnp.zeros_like(weights_out)
    fresh = []
    for f in range(fields):
        for k in range(3):
            weights_out[f, k : k + 1, :] = weights[f][k]
        value = drift[f, 0:count, :]
        for k in range(3):
            value = value + kappas[k : k + count, :] * weights[f][k]
        fresh.append(value)
        if proj_out is not None:
            proj_out[f, 0:count, :] = value
    tent_sums(
        coef,
        following[...],
        [v[0:3] for v in fresh],
        aux,
        vals,
        messages,
        None,
        kappas[1:2, :],
    )


def poly_kernel(steps, resumed, state, coef, heights, stack, *rest):
    rest = list(rest)
    current = rest.pop(0) if resumed else None
    moves = any(mixed is not None for mixed, _ in steps)
    out = rest.pop(0) if moves else None
    left = rest.pop(0) if steps[-1][1] is not None else None
    packed, powers, factors = rest
    fields, basis, n_elem = state.shape
    width = n_elem // HALVES
    half_rows = packed.shape[1] // 2
    written = set()
    packed[...] = jnp.zeros_like(packed)

    def multiply(f, half, target):
        source = out if half in written else state
        high, low = split(source[f, :, half * width : (half + 1) * width])
        slot = f % 2
        packed[slot, 0:basis, :] = high
        packed[slot, half_rows : half_rows + basis, :] = low
        product = jnp.dot(stack[...], packed[slot], preferred_element_type=F32)
        target[f] = product[: 3 * half_rows] + product[3 * half_rows :]

    def set_factors(level, half):
        at = slice(half * width, (half + 1) * width)
        height = heights[level : level + 1, at]
        for g in range(fields):
            for f in range(fields):
                factors[g * fields + f] = jnp.broadcast_to(
                    height * coef[g, f : f + 1, at], (8, width)
                )

    def mix_lines(half, groups, values):
        base = out if half in written else state
        for tile in range(width // 128):
            near = slice(tile * 128, (tile + 1) * 128)
            at = slice(half * width + tile * 128, half * width + (tile + 1) * 128)
            factor = [factors[k, :, near] for k in range(fields * fields)]

            def combine(start, values):
                mixed = []
                for g in range(fields):
                    total = start[g]
                    for f in range(fields):
                        total = total + factor[g * fields + f] * values[f]
                    mixed.append(total)
                return mixed

            for group in groups:
                lines = slice(group * 8, group * 8 + 8)

                def power(k):
                    rows = slice(k * half_rows + group * 8, k * half_rows + group * 8 + 8)
                    return [values[f, rows, near] for f in range(fields)]

                value = combine(power(1), power(2))
                value = combine(power(0), value)
                value = combine([base[f, lines, at] for f in range(fields)], value)
                for f in range(fields):
                    out[f, lines, at] = value[f]

    groups = basis // 8 // fields
    for index, (mixed, multiplied) in enumerate(steps):
        last = index == len(steps) - 1
        target = left if last else powers.at[index % 2]
        if mixed is not None:
            set_factors(*mixed)
        for f in range(fields):
            if multiplied is not None:
                multiply(f, multiplied[1], target)
            if mixed is not None:
                mix_lines(mixed[1], range(f * groups, (f + 1) * groups), current)
        if mixed is not None:
            written.add(mixed[1])
        current = target
    for half in range(HALVES if moves else 0):
        if half not in written:
            at = slice(half * width, (half + 1) * width)
            out[:, :, at] = state[:, :, at]


def advance(coef, height, held, count):
    fields = coef.shape[0]
    value = mix(coef, [held[f, 5 : 5 + count, :] for f in range(fields)])
    value = [held[f, 6 : 6 + count, :] + height / 3.0 * value[f] for f in range(fields)]
    value = mix(coef, value)
    value = [held[f, 7 : 7 + count, :] + height / 2.0 * value[f] for f in range(fields)]
    value = mix(coef, value)
    return [held[f, 8 : 8 + count, :] + height * value[f] for f in range(fields)]


def lift_kernel(coef, heights, weights0, weights1, lcols, state, out, wide, held):
    fields, basis, _ = out.shape
    for k in range(3):
        wide[k] = jnp.broadcast_to(lcols[:, k : k + 1], (basis, 128))
    held[...] = jnp.zeros_like(held)
    for f in range(fields):
        held[f, 8:11, :] = weights0[f, 0:3, :]
    value = advance(coef, heights[1:2, :], held, 6)
    for f in range(fields):
        held[f, 8:14, :] = value[f]
        held[f, 8:11, :] = held[f, 8:11, :] + weights1[f, 0:3, :]
    value = advance(coef, heights[2:3, :], held, 9)
    high, low = split(lcols[...])
    left = jnp.concatenate([high, high, low], axis=1)
    for f in range(fields):
        held[f, 8:17, :] = value[f]
        right_high, right_low = split(held[f, 8:24, :])
        right = jnp.concatenate([right_high, right_low, right_high], axis=0)
        out[f] = state[f] + jnp.dot(left, right, preferred_element_type=F32)


def closing_kernel(level, coef, heights, kappas, old_aux, wide, state, member, *rest):
    tables = rest[:SLOTS]
    out, table, held, scales, sems = rest[SLOTS:]
    fields, basis, n_elem = state.shape
    means = gather([t[...] for t in tables], table, member[...])
    height = heights[level : level + 1, :]
    weights = lift_weights(coef, height, means, old_aux, kappas)
    for f in range(fields):
        for k in range(3):
            scales[f, k : k + 1, :] = weights[f][k]

    def field(f, carry):
        for pair in range(n_elem // 256):
            lanes = [
                slice(pair * 256 + part * 128, pair * 256 + part * 128 + 128) for part in range(2)
            ]
            scale = [
                [jnp.broadcast_to(scales[f, k : k + 1, at], (8, 128)) for k in range(3)]
                for at in lanes
            ]
            for group in range(basis // 8):
                lines = slice(group * 8, group * 8 + 8)
                vector = [wide[k, lines, :] for k in range(3)]
                for part in range(2):
                    value = state[f, lines, lanes[part]]
                    for k in range(3):
                        value = value + vector[k] * scale[part][k]
                    held[f, lines, lanes[part]] = value
        pltpu.make_async_copy(held.at[f], out.at[f], sems.at[f]).start()
        return carry

    lax.fori_loop(0, fields, field, 0)
    for f in range(fields):
        pltpu.make_async_copy(held.at[f], out.at[f], sems.at[f]).wait()


def call(kernel, outs, args, scratch=(), scalars=0, flops=1000000, space=pltpu.VMEM, out_space=pltpu.VMEM, limit=40):
    specs = [
        pl.BlockSpec(memory_space=pltpu.SMEM if i < scalars else space)
        for i in range(len(args))
    ]
    single = not isinstance(outs, (list, tuple))
    shapes = [outs] if single else list(outs)
    moved = sum(4 * s.size for s in shapes) + sum(4 * a.size for a in args)
    result = pl.pallas_call(
        kernel,
        out_shape=shapes,
        in_specs=specs,
        out_specs=[pl.BlockSpec(memory_space=out_space)] * len(shapes),
        scratch_shapes=list(scratch),
        cost_estimate=pl.CostEstimate(flops=flops, bytes_accessed=moved, transcendentals=0),
        compiler_params=pltpu.CompilerParams(vmem_limit_bytes=min(limit * 1024 * 1024, 67043328)),
    )(*args)
    return result[0] if single else result


def shaped(*dims, dtype=F32):
    return jax.ShapeDtypeStruct(dims, dtype)


def swap(x, axis, odd):
    size = lax.axis_size(axis)
    pairs = []
    for i in range(size):
        mate = (i - 1 + 2 * (i % 2)) % size if odd else i + 1 - 2 * (i % 2)
        pairs.append((i, mate))
    return lax.ppermute(x, axis, pairs)


ROUTES = ((1, "gx", True), (0, "gx", False), (3, "gy", True), (2, "gy", False))


def exchange(pieces):
    received = [None] * 4
    for slot, axis, odd in ROUTES:
        received[slot] = swap(pieces[slot], axis, odd)
    return received


PARTS = ((0, 1), (1, 3), (3, 4), (4, 6), (6, 7))


def poly_steps(levels):
    blocks = [(level, half) for level in range(levels) for half in range(HALVES)]
    return list(zip([None] + blocks, blocks + [None]))


def slab(state, coef, basis_quad, test_deriv, trace_vec, lift_vec, tent_height, elem_tent):
    size_first = lax.axis_size("gx")
    size_second = lax.axis_size("gy")
    fields, basis, n_elem = state.shape
    levels, tent_dev = tent_height.shape
    shape = (size_first, size_second, tent_dev)
    me = (lax.axis_index("gx") * size_second + lax.axis_index("gy")).reshape(1)
    message = [shaped(ROWS // 2, 2 * tent_dev)] * SLOTS
    aux_shape = shaped(BACK, n_elem)
    vals = pltpu.VMEM((ROWS, n_elem), F32)
    table = pltpu.VMEM((BACK, SLOTS * tent_dev), F32)

    kept = [
        shaped(*basis_quad.shape),
        shaped(*test_deriv.shape[::-1]),
        shaped(*state.shape),
        shaped(*coef.shape),
        shaped(*elem_tent.shape, dtype=jnp.int32),
    ]
    rows3, lift, aux, *out = call(
        functools.partial(opening_kernel, shape),
        [shaped(8, basis), shaped(1, basis), aux_shape] + message + kept,
        (
            me,
            *(
                pltpu.with_memory_space_constraint(x, pltpu.HBM)
                for x in (
                    basis_quad,
                    test_deriv.T,
                    trace_vec,
                    lift_vec,
                    state,
                    coef,
                    tent_height,
                    elem_tent,
                )
            ),
        ),
        [
            vals,
            pltpu.VMEM(trace_vec.shape, F32),
            pltpu.VMEM(lift_vec.shape, F32),
            pltpu.VMEM(tent_height.shape, F32),
            pltpu.VMEM((3, basis, 128), F32),
            pltpu.VMEM((fields, 8, n_elem), F32),
            pltpu.SemaphoreType.DMA((8,)),
        ],
        1,
        space=pltpu.HBM,
    )
    basis_near, test_near, state, coef, elem_tent = out[SLOTS:]
    out = out[:SLOTS]
    stack, rstack, lcols, kappas = call(
        powers_kernel,
        [
            shaped(768, 256, dtype=BF16),
            shaped(32, 256, dtype=BF16),
            shaped(basis, 16),
            shaped(16, n_elem),
        ],
        (basis_near, test_near, rows3, lift),
        [
            pltpu.VMEM((16, basis), F32),
            pltpu.VMEM((8 + 2 * basis, basis), F32),
            pltpu.VMEM((basis, basis + 8), F32),
        ],
        flops=100000000,
    )
    proj = call(
        projections_kernel,
        shaped(fields, 16, n_elem),
        (rstack, state),
        [pltpu.VMEM((256, 256), BF16)],
        flops=300000000,
    )
    width = n_elem // HALVES
    weights = []
    heights = None
    steps = poly_steps(levels)
    values = state
    held = []

    def advance_state(values, held, part):
        chosen = PARTS[part]
        resumed = chosen[0] > 0
        mine = steps[chosen[0] : chosen[1]]
        half_powers = shaped(fields, 384, width)
        moves = any(mixed is not None for mixed, _ in mine)
        outs = [shaped(fields, basis, n_elem)] if moves else []
        if mine[-1][1] is not None:
            outs.append(half_powers)
        held = call(
            functools.partial(poly_kernel, mine, resumed),
            outs,
            (values, coef, heights, stack, *held),
            [
                pltpu.VMEM((2, 256, width), BF16),
                pltpu.VMEM((2, fields, 384, width), F32),
                pltpu.VMEM((fields * fields, 8, width), F32),
            ],
            flops=3000000000,
        )
        if moves:
            values, *held = held
        return values, held

    for level in range(levels):
        received = exchange(out[:4])
        means = call(owner_kernel, shaped(BACK, tent_dev), (kappas, out[4], *received))
        back = exchange([means] * 4)
        if level == 0:
            memberships = call(
                functools.partial(members_kernel, shape),
                [shaped(SLOTS * tent_dev, n_elem, dtype=BF16)] * levels,
                (me, elem_tent),
                (),
                1,
            )
            heights = call(
                lambda *refs: heights_kernel(refs[:5], refs[5 : 5 + levels], *refs[5 + levels :]),
                shaped(8, n_elem),
                (*received, out[4], *memberships),
                [table],
                flops=10000000,
            )
        if level < levels - 1:
            count = 6 - 3 * level
            drift = call(
                functools.partial(drift_kernel, level, count),
                shaped(fields, 8, n_elem),
                (coef, heights, proj),
            )
        if level < levels - 1:
            more = [shaped(fields, 8, n_elem)] if level < levels - 2 else []
            weight, aux, *out = call(
                functools.partial(element_kernel, level, count),
                [shaped(fields, 8, n_elem), aux_shape] + message + more,
                (
                    coef,
                    heights,
                    kappas,
                    aux,
                    drift,
                    memberships[level],
                    memberships[level + 1],
                    *back,
                    means,
                ),
                [vals, table],
            )
            weights.append(weight)
            if more:
                proj = out.pop()
    for part in range(len(PARTS)):
        values, held = advance_state(values, held, part)
    values, wide = call(
        lift_kernel,
        [shaped(fields, basis, n_elem), shaped(3, basis, 128)],
        (coef, heights, weights[0], weights[1], lcols, values),
        [pltpu.VMEM((fields, 24, n_elem), F32)],
        flops=100000000,
    )
    return call(
        functools.partial(closing_kernel, levels - 1),
        shaped(fields, basis, n_elem),
        (coef, heights, kappas, aux, wide, values, memberships[levels - 1], *back, means),
        [
            table,
            pltpu.VMEM(state.shape, F32),
            pltpu.VMEM((fields, 8, n_elem), F32),
            pltpu.SemaphoreType.DMA((fields,)),
        ],
        out_space=pltpu.HBM,
    )


def solution(mesh):
    placed = (
        P(None, None, ("gx", "gy")),
        P(None, None, ("gx", "gy")),
        P(),
        P(),
        P(),
        P(),
        P(None, ("gx", "gy")),
        P(None, ("gx", "gy")),
    )
    return jax.shard_map(
        slab,
        mesh=mesh,
        in_specs=placed,
        out_specs=P(None, None, ("gx", "gy")),
        check_vma=False,
    )
```
